128 devices in a mesh: grp: 8 (over x, core), dev: 16 (over y, z).
Axes of the slice: x: 4, y: 4, z: 4, core: 2. Of those that a mesh axis runs over, the one named last changes fastest.
Arguments:
- parent_state: float32 [24, 512, 2048], P(None, 'grp', 'dev'), may hold values from -6 to 6
- nest_state: float32 [16, 24, 384, 384], P('grp', None, 'dev'), may hold values from -6 to 6
- nest_anchor: int32 [16, 2], replicated, may hold values from 0 to 1920, as said below
- diffusion: float32 [2, 24], replicated, may hold values from 0.02 to 0.05
- courant: float32 [2, 24], replicated, may hold values from 0.05 to 0.15
Outputs:
- parent_out: float32 [24, 512, 2048], P(None, 'grp', 'dev')
- nest_out: float32 [16, 24, 384, 384], P('grp', None, 'dev')
The draws below stay inside these ranges and needn't reach their ends.
Inputs may be any that keep to these rules, and one draw needn't show every extreme that they name: `nest_anchor`: the parent grid is cut into 2 x 16 / 2 disjoint bands of 256 x 256 cells; each nest lies in a band of its own, its 128 x 128 covered cells inside that band.
All inputs are finite; a program needn't handle non-finite values.
Results may differ from the reference program's by a relative error of at most 0.0003.
Values sent between devices are 32-bit elements; how exact they have to be, the bound alone decides.
A program may use at most 320 MiB of HBM per device.

```python
import jax
import jax.numpy as jnp
from jax import lax

NCOL = 384
C = 24
NESTS = 16
PY = 512
PX = 2048
NROWS = 384
FP_R = 128
FP_C = 128
BAND_R = 256
BAND_C = 256


def draw_nest_anchor(key, part):
    band_key, row_key, col_key = jax.random.split(key, 3)
    band_order = jax.random.permutation(band_key, NESTS)
    band_row = band_order // (NESTS // 2)
    band_col = band_order % (NESTS // 2)
    offset_row = jax.random.randint(row_key, (NESTS,), 0, BAND_R - FP_R + 1)
    offset_col = jax.random.randint(col_key, (NESTS,), 0, BAND_C - FP_C + 1)
    return jnp.stack([band_row * BAND_R + offset_row, band_col * BAND_C + offset_col], axis=1).astype(jnp.int32)


def levels(key, dims, cuts, least, top_value):
    loudness, own = 1.0, jax.random.fold_in(key, 6)
    for position, parts in cuts:
        heights = jnp.exp(jax.random.uniform(jax.random.fold_in(own, position), (parts,), jnp.float32, least / len(cuts), top_value / len(cuts)))
        loudness = loudness * jnp.repeat(heights, dims[position] // parts).reshape([-1 if axis == position else 1 for axis in range(len(dims))])
    return loudness


def gaussian(rng, shape, deviation, limit, shards=(), held_as=jnp.bfloat16):
    drawn = deviation * jax.random.normal(rng, shape, jnp.float32)
    if shards:
        drawn = drawn * levels(rng, shape, shards, -0.22, 0.18)
    return jnp.clip(drawn, -limit, limit).astype(held_as)


def setup_inputs(seed: int = 0) -> dict:
    arg_keys = jax.random.split(jax.random.key(seed), 6)
    parent_state = gaussian(arg_keys[0], (C, PY, PX), 1.0, 6.0, ((1, 8), (2, 16)), jnp.float32)
    nest_state = gaussian(arg_keys[1], (NESTS, C, NROWS, NCOL), 1.0, 6.0, ((0, 8), (2, 16)), jnp.float32)
    nest_anchor = draw_nest_anchor(jax.random.fold_in(arg_keys[5], 71), 0)
    diffusion = jnp.clip(jax.random.uniform(arg_keys[3], (2, C), jnp.float32, 0.02, 0.05), 0.02, 0.05)
    courant = jnp.clip(jax.random.uniform(arg_keys[4], (2, C), jnp.float32, 0.05, 0.15), 0.05, 0.15)
    return dict(parent_state=parent_state, nest_state=nest_state, nest_anchor=nest_anchor, diffusion=diffusion, courant=courant)


def stencil(padded, diff_x, diff_y, adv_x, adv_y):
    centre = padded[..., 1:-1, 1:-1]
    eastern = padded[..., 1:-1, 2:]
    western = padded[..., 1:-1, :-2]
    northern = padded[..., 2:, 1:-1]
    southern = padded[..., :-2, 1:-1]
    return (centre + diff_x * (eastern - 2.0 * centre + western)
            + diff_y * (northern - 2.0 * centre + southern)
            - adv_x * (centre - western) - adv_y * (centre - southern))


def reference(parent_state, nest_state, nest_anchor, diffusion, courant):
    channels = parent_state.shape[0]
    diff_x = diffusion[0][:, None, None]
    diff_y = diffusion[1][:, None, None]
    adv_x = courant[0][:, None, None]
    adv_y = courant[1][:, None, None]
    parent_pad = jnp.pad(parent_state, ((0, 0), (1, 1), (1, 1)))
    advanced = stencil(parent_pad, diff_x, diff_y, adv_x, adv_y)

    def one_nest(inputs):
        fine_field, anchor = inputs
        row_start = anchor[0].astype(jnp.int32)
        col_start = anchor[1].astype(jnp.int32)
        zero_start = jnp.zeros((), jnp.int32)
        west_cycle = lax.dynamic_slice(parent_pad, (zero_start, row_start + 1, col_start), (channels, FP_R, 1))[:, :, 0]
        east_cycle = lax.dynamic_slice(parent_pad, (zero_start, row_start + 1, col_start + FP_C + 1), (channels, FP_R, 1))[:, :, 0]
        south_cycle = lax.dynamic_slice(parent_pad, (zero_start, row_start, col_start + 1), (channels, 1, FP_C))[:, 0, :]
        north_cycle = lax.dynamic_slice(parent_pad, (zero_start, row_start + FP_R + 1, col_start + 1), (channels, 1, FP_C))[:, 0, :]
        west_fine = jnp.repeat(west_cycle, 3, axis=1)
        east_fine = jnp.repeat(east_cycle, 3, axis=1)
        corner = jnp.zeros((channels, 1), jnp.float32)
        top_row = jnp.concatenate([corner, jnp.repeat(south_cycle, 3, axis=1), corner], axis=1)[:, None, :]
        bottom = jnp.concatenate([corner, jnp.repeat(north_cycle, 3, axis=1), corner], axis=1)[:, None, :]
        for substep in range(3):
            middle = jnp.concatenate([west_fine[:, :, None], fine_field, east_fine[:, :, None]], axis=2)
            padded = jnp.concatenate([top_row, middle, bottom], axis=1)
            fine_field = stencil(padded, 3.0 * diff_x, 3.0 * diff_y, adv_x, adv_y)
        average = fine_field.reshape(channels, FP_R, 3, FP_C, 3).mean(axis=(2, 4))
        return fine_field, average

    nest_out, averages = lax.map(one_nest, (nest_state, nest_anchor))

    def place(nest_index, parent_field):
        return lax.dynamic_update_slice(
            parent_field, averages[nest_index],
            (jnp.zeros((), jnp.int32), nest_anchor[nest_index, 0], nest_anchor[nest_index, 1]))

    parent_out = lax.fori_loop(0, NESTS, place, advanced)
    return parent_out, nest_out
```

```python
import functools

import jax
import jax.numpy as jnp
from jax import lax
from jax.experimental import pallas as pl
from jax.experimental.pallas import tpu as pltpu
from jax.sharding import PartitionSpec as P

F32 = jnp.float32
BF16 = jnp.bfloat16
I32 = jnp.int32
MESH = pl.DeviceIdType.MESH

G = 8
D = 16
C = 24
CH = C // 2
TR = 64
TC = 128
NR = 24
NC = 384
FP = 128
BAND = 256
NESTS = 16
PLANES = 2 * C
WR = NR + 16
LEAD = 8


def iota(shape, axis):
    return lax.broadcasted_iota(I32, shape, axis)


def remote(src, dst, send, recv, axis, target):
    return pltpu.make_async_remote_copy(
        src_ref=src,
        dst_ref=dst,
        send_sem=send,
        recv_sem=recv,
        device_id={axis: target},
        device_id_type=MESH,
    )


def split3(a):
    hi = a.astype(BF16)
    rest = a - hi.astype(F32)
    mid = rest.astype(BF16)
    return hi, mid, (rest - mid.astype(F32)).astype(BF16)


def kernel(
    anchor,
    diff,
    cour,
    parent,
    nest,
    pout,
    nout,
    work,
    pv,
    prow_in,
    pcol,
    pcol_in,
    item,
    item_in,
    wecol,
    strip,
    strip_in,
    edge,
    edge_in,
    ghost,
    fine,
    colsum,
    avg,
    slabs,
    slab_out,
    canvas,
    half,
    half_in,
    adv,
    tab,
    local_sem,
    halo_sem,
    item_sem,
    strip_sem,
    edge_sem,
    slab_sem,
    canvas_sem,
    half_sem,
):
    g = lax.axis_index("grp")
    d = lax.axis_index("dev")
    core = g % 2
    row0 = g * TR
    col0 = d * TC
    lane = iota((1, 128), 1)

    own_nest = pltpu.make_async_copy(nest, work.at[:, pl.ds(8, NR), :], local_sem.at[0])
    own_nest.start()
    own_parent = pltpu.make_async_copy(parent, pv, local_sem.at[1])
    own_parent.start()

    barrier = pltpu.get_barrier_semaphore()
    for k in range(1, G):
        pl.semaphore_signal(barrier, inc=1, device_id={"grp": (g + k) % G}, device_id_type=MESH)
    for k in range(1, D):
        pl.semaphore_signal(barrier, inc=1, device_id={"dev": (d + k) % D}, device_id_type=MESH)

    key = [anchor[n, 0] // BAND * 8 + anchor[n, 1] // BAND for n in range(NESTS)]
    band_row = g // 4
    for b in range(8):
        found = jnp.int32(0)
        for n in range(NESTS):
            found = jnp.where(key[n] == band_row * 8 + b, n, found)
        tab[b] = found
    other = jnp.int32(0)
    for n in range(NESTS):
        other = jnp.where(key[n] == (1 - band_row) * 8 + d // 2, n, other)
    mine = tab[d // 2]
    odd = d % 2
    beside = tab[jnp.clip(d // 2 - 1 + 2 * odd, 0, 7)]

    r_m, q_m = anchor[mine, 0], anchor[mine, 1]
    west_m = q_m - 1 - col0
    east_m = q_m + FP - col0
    is_west = (west_m >= 0) & (west_m < TC)
    is_east = (east_m >= 0) & (east_m < TC)
    pick = jnp.where(is_west, west_m, jnp.where(is_east, east_m, 0))
    q_b = anchor[beside, 1]
    beside_on = jnp.where(odd == 1, q_b == col0 + TC, q_b + FP == col0)

    south_m = r_m - 1 - row0
    north_m = r_m + FP - row0
    is_south = (south_m >= 0) & (south_m < TR)
    is_north = (north_m >= 0) & (north_m < TR)
    row_pick = jnp.where(is_south, south_m, jnp.where(is_north, north_m, 0))
    r_o, q_o = anchor[other, 0], anchor[other, 1]
    low = band_row == 0
    other_on = jnp.where(low, r_o == row0 + TR, r_o + FP == row0)

    own_parent.wait()

    def gather(c, carry):
        first, last, picked, row_m, row_o = carry
        x = pv[c]
        here = lane == c
        first = jnp.where(here, pltpu.roll(x, c, 1), first)
        last = jnp.where(here, pltpu.roll(x, c + 1, 1), last)
        picked = jnp.where(here, pltpu.roll(x, (c - pick) & 127, 1), picked)
        sub = iota((C, 128), 0) == c
        row_m = jnp.where(sub, pv[c, pl.ds(row_pick, 1), :], row_m)
        edge_row = jnp.where(low, x[TR - 1 : TR], x[0:1])
        row_o = jnp.where(sub, edge_row, row_o)
        return first, last, picked, row_m, row_o

    zero_col = jnp.zeros((TR, 128), F32)
    zero_row = jnp.zeros((C, 128), F32)
    first, last, picked, row_m, row_o = lax.fori_loop(
        0, C, gather, (zero_col, zero_col, zero_col, zero_row, zero_row)
    )
    pcol[0] = first
    pcol[1] = last
    side = jnp.where(odd == 1, last, first)
    place_m = (mine % 2) * 48 + jnp.where(is_west, 0, C)
    place_b = (beside % 2) * 48 + jnp.where(odd == 1, 0, C)
    cols_m = pltpu.roll(picked, place_m, 1)
    cols_b = pltpu.roll(side, place_b, 1)
    span_m = lane + (q_m - col0)
    span_o = lane + (q_o - col0)
    rows_m = jnp.where((span_m >= 0) & (span_m < TC), pltpu.roll(row_m, (col0 - q_m) & 127, 1), 0.0)
    rows_o = jnp.where((span_o >= 0) & (span_o < TC), pltpu.roll(row_o, (col0 - q_o) & 127, 1), 0.0)
    for t in range(G):
        a_m = jnp.where((mine // 2 == t) & (is_west | is_east), 1, 0)
        a_b = jnp.where((beside // 2 == t) & beside_on, 1, 0)
        item[t, pl.ds(0, TR), :] = jnp.where(a_m == 1, cols_m, 0.0) + jnp.where(a_b == 1, cols_b, 0.0)
        for a in range(2):
            s_m = jnp.where((mine == 2 * t + a) & (is_south | is_north), 1, 0)
            s_o = jnp.where((other == 2 * t + a) & other_on, 1, 0)
            item[t, pl.ds(TR + C * a, C), :] = jnp.where(s_m == 1, rows_m, 0.0) + jnp.where(
                s_o == 1, rows_o, 0.0
            )

    pl.semaphore_wait(barrier, G + D - 2)

    sends = []
    for k in range(1, G):
        t = (g + k) % G
        cp = remote(item.at[t], item_in.at[g], item_sem.at[0, k], item_sem.at[1, k], "grp", t)
        cp.start()
        sends.append(cp)
    up_g, dn_g = (g + 1) % G, (g + G - 1) % G
    up_d, dn_d = (d + 1) % D, (d + D - 1) % D
    halos = [
        remote(parent.at[:, pl.ds(TR - 1, 1), :], prow_in.at[0, :, pl.ds(0, 1), :], halo_sem.at[0, 0], halo_sem.at[1, 0], "grp", up_g),
        remote(parent.at[:, pl.ds(0, 1), :], prow_in.at[1, :, pl.ds(0, 1), :], halo_sem.at[0, 1], halo_sem.at[1, 1], "grp", dn_g),
        remote(pcol.at[1], pcol_in.at[0], halo_sem.at[0, 2], halo_sem.at[1, 2], "dev", up_d),
        remote(pcol.at[0], pcol_in.at[1], halo_sem.at[0, 3], halo_sem.at[1, 3], "dev", dn_d),
        remote(nest.at[:, pl.ds(NR - 3, 3), :], work.at[:, pl.ds(5, 3), :], halo_sem.at[0, 4], halo_sem.at[1, 4], "dev", up_d),
        remote(nest.at[:, pl.ds(0, 3), :], work.at[:, pl.ds(8 + NR, 3), :], halo_sem.at[0, 5], halo_sem.at[1, 5], "dev", dn_d),
    ]
    for cp in halos:
        cp.start()

    item_in[g] = item[g]

    for k in range(1, G):
        s = (g + G - k) % G
        remote(item.at[s], item_in.at[s], item_sem.at[0, k], item_sem.at[1, k], "grp", s).wait_recv()
    wecol[pl.ds(0, LEAD), :] = jnp.zeros((LEAD, 128), F32)
    wecol[pl.ds(LEAD + G * TR, 32), :] = jnp.zeros((32, 128), F32)
    south = [jnp.zeros((C, 128), F32)] * 2
    north = [jnp.zeros((C, 128), F32)] * 2
    r_own = [anchor[2 * g + a, 0] for a in range(2)]
    for s in range(G):
        wecol[pl.ds(LEAD + s * TR, TR), :] = item_in[s, pl.ds(0, TR), :]
        for a in range(2):
            got = item_in[s, pl.ds(TR + C * a, C), :]
            below = r_own[a] - 1 - s * TR
            above = r_own[a] + FP - s * TR
            south[a] = south[a] + jnp.where((below >= 0) & (below < TR), got, 0.0)
            north[a] = north[a] + jnp.where((above >= 0) & (above < TR), got, 0.0)
    for a in range(2):
        edge[0, pl.ds(C * a, C), :] = south[a]
        edge[1, pl.ds(C * a, C), :] = north[a]

    def strip_of(t):
        parts = [wecol[pl.ds(LEAD - 1 + r_own[a] + 8 * t, 16), :] for a in range(2)]
        return jnp.where(lane < 48, parts[0], parts[1])

    for k in range(1, D):
        t = (d + k) % D
        strip[k] = strip_of(t)
        cp = remote(strip.at[k], strip_in.at[k], strip_sem.at[0, k], strip_sem.at[1, k], "dev", t)
        cp.start()
        sends.append(cp)
    strip_in[0] = strip_of(d)

    for e, end in ((0, 0), (1, D - 1)):

        @pl.when(d != end)
        def _(e=e, end=end):
            remote(edge.at[e], edge_in.at[d], edge_sem.at[0, e], edge_sem.at[1, d], "dev", end).start()

    for cp in halos[:4]:
        cp.wait()
    tile = iota((TR, 128), 0)

    def parent_step(c, _):
        mid = pv[c]
        kx, ky = diff[0, c], diff[1, c]
        ax, ay = cour[0, c], cour[1, c]
        gw = jnp.where(d == 0, 0.0, pltpu.roll(pcol_in[0], (128 - c) & 127, 1))
        ge = jnp.where(d == D - 1, 0.0, pltpu.roll(pcol_in[1], 127 - c, 1))
        gs = jnp.where(g == 0, 0.0, prow_in[0, c, 0:1, :])
        gn = jnp.where(g == G - 1, 0.0, prow_in[1, c, 0:1, :])
        west = jnp.where(lane == 0, gw, pltpu.roll(mid, 1, 1))
        east = jnp.where(lane == 127, ge, pltpu.roll(mid, 127, 1))
        below = jnp.where(tile == 0, gs, pltpu.roll(mid, 1, 0))
        above = jnp.where(tile == TR - 1, gn, pltpu.roll(mid, TR - 1, 0))
        adv[c] = (
            mid * (1.0 - 2.0 * kx - 2.0 * ky - ax - ay)
            + kx * east
            + (kx + ax) * west
            + ky * above
            + (ky + ay) * below
        )
        return 0

    lax.fori_loop(0, C, parent_step, 0)

    for k in range(1, D):
        remote(strip.at[k], strip_in.at[k], strip_sem.at[0, k], strip_sem.at[1, k], "dev", d).wait_recv()
    total = strip_in[0]
    for k in range(1, D):
        total = total + strip_in[k]
    for i in range(10):
        ghost[pl.ds(5 + 3 * i, 3), :] = jnp.broadcast_to(total[i : i + 1], (3, 128))

    for e, end in ((0, 0), (1, D - 1)):

        @pl.when(d == end)
        def _(e=e, end=end):
            whole = edge[e]
            for k in range(1, D):
                s = (end + k) % D
                remote(edge.at[e], edge_in.at[s], edge_sem.at[0, e], edge_sem.at[1, s], "dev", end).wait_recv()
            for k in range(1, D):
                whole = whole + edge_in[(end + k) % D]
            off = iota((TC, NC), 1) - 3 * iota((TC, NC), 0)
            spread = jnp.where((off >= 0) & (off < 3), 1.0, 0.0).astype(BF16)
            spread_out = sum(
                jnp.dot(part, spread, preferred_element_type=F32) for part in split3(whole)
            )
            for j in range(3):
                fine[j] = spread_out[:, 128 * j : 128 * j + 128]

        @pl.when(d != end)
        def _(e=e, end=end):
            remote(edge.at[e], edge_in.at[d], edge_sem.at[0, e], edge_sem.at[1, d], "dev", end).wait_send()

    for cp in halos[4:]:
        cp.wait()
    own_nest.wait()

    off = iota((NC, TC), 0) - 3 * iota((NC, TC), 1)
    collect = jnp.where((off >= 0) & (off < 3), 1.0, 0.0).astype(BF16)
    fine_row = iota((WR, 128), 0)
    fixed = ((fine_row == 7) & (d == 0)) | ((fine_row == 8 + NR) & (d == D - 1))

    def nest_step(p, _):
        c = lax.rem(p, C)
        base = 48 * (p // C) + c
        kx, ky = 3.0 * diff[0, c], 3.0 * diff[1, c]
        ax, ay = cour[0, c], cour[1, c]
        k_c, k_w, k_s = 1.0 - 2.0 * kx - 2.0 * ky - ax - ay, kx + ax, ky + ay
        cols = ghost[...]
        gw = pltpu.roll(cols, lax.rem(128 - base, 128), 1)
        ge = pltpu.roll(cols, 127 - C - base, 1)
        x = [work[p, :, pl.ds(128 * j, 128)] for j in range(3)]
        held = [fine[j, pl.ds(p, 1), :] for j in range(3)]
        for step in range(3):
            x = [jnp.where(fixed, held[j], x[j]) for j in range(3)]
            right = [gw] + [pltpu.roll(v, 1, 1) for v in x]
            left = [pltpu.roll(v, 127, 1) for v in x] + [ge]
            x = [
                k_c * x[j]
                + kx * jnp.where(lane == 127, left[j + 1], left[j])
                + k_w * jnp.where(lane == 0, right[j], right[j + 1])
                + ky * pltpu.roll(x[j], WR - 1, 0)
                + k_s * pltpu.roll(x[j], 1, 0)
                for j in range(3)
            ]
        for j in range(3):
            work[p, pl.ds(8, NR), pl.ds(128 * j, 128)] = x[j][8 : 8 + NR]
        return 0

    lax.fori_loop(0, PLANES, nest_step, 0)
    done_nest = pltpu.make_async_copy(work.at[:, pl.ds(8, NR), :], nout, local_sem.at[0])
    done_nest.start()

    def sum_cols(b, _):
        x = jnp.concatenate([work[8 * b + i, pl.ds(8, NR), :] for i in range(8)], axis=0)
        hi = x.astype(BF16)
        lo = (x - hi.astype(F32)).astype(BF16)
        colsum[pl.ds(pl.multiple_of(b * 8 * NR, 8 * NR), 8 * NR), :] = jnp.dot(
            hi, collect, preferred_element_type=F32
        ) + jnp.dot(lo, collect, preferred_element_type=F32)
        return 0

    lax.fori_loop(0, PLANES // 8, sum_cols, 0)
    mean = sum(colsum[pl.ds(k, PLANES * 8, stride=3), :] for k in range(3)) * (1.0 / 9.0)
    avg[...] = mean.reshape(2, C, 8, 128)

    for k in range(1, G):
        t = (g + k) % G
        cp = remote(
            avg.at[:, pl.ds(CH * (t % 2), CH)],
            slabs.at[pl.ds(2 * g, 2)],
            slab_sem.at[0, k],
            slab_sem.at[1, k],
            "grp",
            t,
        )
        cp.start()
        sends.append(cp)
    slabs[pl.ds(2 * g, 2)] = avg[:, pl.ds(CH * core, CH)]
    for k in range(1, G):
        s = (g + G - k) % G
        remote(
            avg.at[:, pl.ds(0, CH)],
            slabs.at[pl.ds(2 * s, 2)],
            slab_sem.at[0, k],
            slab_sem.at[1, k],
            "grp",
            s,
        ).wait_recv()

    for k in range(1, D):
        t = (d + k) % D
        slab_out[k] = slabs[tab[t // 2]]
        cp = remote(
            slab_out.at[k],
            canvas.at[:, pl.ds(64 + 8 * d, 8), :],
            canvas_sem.at[0, k],
            canvas_sem.at[1, k],
            "dev",
            t,
        )
        cp.start()
        sends.append(cp)
    canvas[:, pl.ds(64 + 8 * d, 8), :] = slabs[mine]
    for k in range(1, D):
        s = (d + D - k) % D
        remote(
            slab_out.at[k],
            canvas.at[:, pl.ds(64 + 8 * s, 8), :],
            canvas_sem.at[0, k],
            canvas_sem.at[1, k],
            "dev",
            s,
        ).wait_recv()

    pair = g + 1 - 2 * core
    pair_row = jnp.clip(pair * TR - r_m, -TR, FP) + TR
    half[...] = canvas[:, pl.ds(pair_row, TR), :]
    swap = remote(half, half_in, half_sem.at[0], half_sem.at[1], "grp", pair)
    swap.start()

    own_row = jnp.clip(row0 - r_m, -TR, FP) + TR
    shift = (q_m - col0) & 127
    tile_row = iota((TR, 128), 0) + (row0 - r_m)
    tile_col = iota((TR, 128), 1) + (col0 - q_m)
    covered = (tile_row >= 0) & (tile_row < FP) & (tile_col >= 0) & (tile_col < FP)

    def put_own(j, _):
        c = CH * core + j
        pv[c] = jnp.where(covered, pltpu.roll(canvas[j, pl.ds(own_row, TR), :], shift, 1), adv[c])
        return 0

    def put_other(j, _):
        c = CH * (1 - core) + j
        pv[c] = jnp.where(covered, pltpu.roll(half_in[j], shift, 1), adv[c])
        return 0

    lax.fori_loop(0, CH, put_own, 0)
    swap.wait()
    lax.fori_loop(0, CH, put_other, 0)
    done_parent = pltpu.make_async_copy(pv, pout, local_sem.at[1])
    done_parent.start()
    for cp in sends:
        cp.wait_send()
    done_nest.wait()
    done_parent.wait()


def shards(parent, nest, anchor, diffusion, courant):
    any_space = pl.BlockSpec(memory_space=pl.ANY)
    scalars = pl.BlockSpec(memory_space=pltpu.SMEM)
    dma = pltpu.SemaphoreType.DMA
    vmem = pltpu.VMEM
    pout, nout = pl.pallas_call(
        kernel,
        out_shape=(
            jax.ShapeDtypeStruct((C, TR, TC), F32),
            jax.ShapeDtypeStruct((PLANES, NR, NC), F32),
        ),
        in_specs=[scalars, scalars, scalars, any_space, any_space],
        out_specs=(any_space, any_space),
        scratch_shapes=[
            vmem((PLANES, WR, NC), F32),
            vmem((C, TR, TC), F32),
            vmem((2, C, 8, TC), F32),
            vmem((2, TR, 128), F32),
            vmem((2, TR, 128), F32),
            vmem((G, TR + PLANES, 128), F32),
            vmem((G, TR + PLANES, 128), F32),
            vmem((LEAD + G * TR + 32, 128), F32),
            vmem((D, 16, 128), F32),
            vmem((D, 16, 128), F32),
            vmem((2, PLANES, 128), F32),
            vmem((D, PLANES, 128), F32),
            vmem((WR, 128), F32),
            vmem((3, PLANES, 128), F32),
            vmem((PLANES * NR, TC), F32),
            vmem((2, C, 8, TC), F32),
            vmem((NESTS, CH, 8, TC), F32),
            vmem((D, CH, 8, TC), F32),
            vmem((CH, 256, TC), F32),
            vmem((CH, TR, TC), F32),
            vmem((CH, TR, TC), F32),
            vmem((C, TR, TC), F32),
            pltpu.SMEM((8,), I32),
            dma((2,)),
            dma((2, 6)),
            dma((2, G)),
            dma((2, D)),
            dma((2, D)),
            dma((2, G)),
            dma((2, D)),
            dma((2,)),
        ],
        compiler_params=pltpu.CompilerParams(
            collective_id=0, has_side_effects=True, vmem_limit_bytes=48 * 1024 * 1024
        ),
    )(anchor, diffusion, courant, parent, nest.reshape(PLANES, NR, NC))
    return pout, nout.reshape(2, C, NR, NC)


def solution(mesh):
    placed = (P(None, "grp", "dev"), P("grp", None, "dev", None), P(), P(), P())
    return jax.shard_map(
        shards,
        mesh=mesh,
        in_specs=placed,
        out_specs=(P(None, "grp", "dev"), P("grp", None, "dev", None)),
        check_vma=False,
    )
```

```python
import functools

import jax
import jax.numpy as jnp
from jax import lax
from jax.experimental import pallas as pl
from jax.experimental.pallas import tpu as pltpu
from jax.sharding import PartitionSpec as P

F32 = jnp.float32
BF16 = jnp.bfloat16
I32 = jnp.int32
MESH = pl.DeviceIdType.MESH

G = 8
D = 16
C = 24
TR = 64
TC = 128
NR = 24
NC = 384
FP = 128
BAND = 256
NESTS = 16
PLANES = 2 * C
LEAD = 8


def iota(shape, axis):
    return lax.broadcasted_iota(I32, shape, axis)


def remote(src, dst, send, recv, axis, target):
    return pltpu.make_async_remote_copy(
        src_ref=src,
        dst_ref=dst,
        send_sem=send,
        recv_sem=recv,
        device_id={axis: target},
        device_id_type=MESH,
    )


def split3(a):
    hi = a.astype(BF16)
    rest = a - hi.astype(F32)
    mid = rest.astype(BF16)
    return hi, mid, (rest - mid.astype(F32)).astype(BF16)


def kernel(
    anchor,
    diff,
    cour,
    parent,
    nest,
    pout,
    nout,
    work,
    res,
    pv,
    prow_in,
    pcol,
    pcol_in,
    item,
    item_in,
    wecol,
    strip,
    strip_in,
    edge,
    edge_in,
    ghost,
    fine,
    coef,
    triple,
    avg,
    slabs0,
    slabs1,
    slabs2,
    slab_out,
    canvas0,
    canvas1,
    canvas2,
    window,
    adv,
    tab,
    row_sem,
    local_sem,
    halo_sem,
    item_sem,
    strip_sem,
    edge_sem,
    slab_sem,
    canvas_sem,
    pair_sem,
):
    slabs = (slabs0, slabs1, slabs2)
    canvas = (canvas0, canvas1, canvas2)
    g = lax.axis_index("grp")
    d = lax.axis_index("dev")
    core = g % 2
    row0 = g * TR
    col0 = d * TC
    lane = iota((1, 128), 1)

    own_parent = pltpu.make_async_copy(parent, pv, local_sem.at[0])
    own_parent.start()
    own_nest = [pltpu.make_async_copy(nest.at[:, r, :], work.at[3 + r], row_sem.at[r]) for r in range(NR)]
    for cp in own_nest:
        cp.start()

    barrier = pltpu.get_barrier_semaphore()
    for k in range(1, G):
        pl.semaphore_signal(barrier, inc=1, device_id={"grp": (g + k) % G}, device_id_type=MESH)
    for k in range(1, D):
        pl.semaphore_signal(barrier, inc=1, device_id={"dev": (d + k) % D}, device_id_type=MESH)

    key = [anchor[n, 0] // BAND * 8 + anchor[n, 1] // BAND for n in range(NESTS)]
    band_row = g // 4
    for b in range(8):
        found = jnp.int32(0)
        for n in range(NESTS):
            found = jnp.where(key[n] == band_row * 8 + b, n, found)
        tab[b] = found
    other = jnp.int32(0)
    for n in range(NESTS):
        other = jnp.where(key[n] == (1 - band_row) * 8 + d // 2, n, other)
    mine = tab[d // 2]
    odd = d % 2
    beside = tab[jnp.clip(d // 2 - 1 + 2 * odd, 0, 7)]

    r_m, q_m = anchor[mine, 0], anchor[mine, 1]
    west_m = q_m - 1 - col0
    east_m = q_m + FP - col0
    is_west = (west_m >= 0) & (west_m < TC)
    is_east = (east_m >= 0) & (east_m < TC)
    pick = jnp.where(is_west, west_m, jnp.where(is_east, east_m, 0))
    q_b = anchor[beside, 1]
    beside_on = jnp.where(odd == 1, q_b == col0 + TC, q_b + FP == col0)

    south_m = r_m - 1 - row0
    north_m = r_m + FP - row0
    is_south = (south_m >= 0) & (south_m < TR)
    is_north = (north_m >= 0) & (north_m < TR)
    row_pick = jnp.where(is_south, south_m, jnp.where(is_north, north_m, 0))
    r_o, q_o = anchor[other, 0], anchor[other, 1]
    low = band_row == 0
    other_on = jnp.where(low, r_o == row0 + TR, r_o + FP == row0)

    for c in range(C):
        kx, ky = 3.0 * diff[0, c], 3.0 * diff[1, c]
        ax, ay = cour[0, c], cour[1, c]
        for i, v in enumerate((1.0 - 2.0 * kx - 2.0 * ky - ax - ay, kx, kx + ax, ky, ky + ay)):
            coef[i, pl.ds(c, 1), :] = jnp.full((1, 128), v, F32)

    own_parent.wait()

    def gather(c, carry):
        first, last, picked, row_m, row_o = carry
        x = pv[c]
        here = lane == c
        first = jnp.where(here, pltpu.roll(x, c, 1), first)
        last = jnp.where(here, pltpu.roll(x, c + 1, 1), last)
        picked = jnp.where(here, pltpu.roll(x, (c - pick) & 127, 1), picked)
        sub = iota((C, 128), 0) == c
        row_m = jnp.where(sub, pv[c, pl.ds(row_pick, 1), :], row_m)
        edge_row = jnp.where(low, x[TR - 1 : TR], x[0:1])
        row_o = jnp.where(sub, edge_row, row_o)
        return first, last, picked, row_m, row_o

    zero_col = jnp.zeros((TR, 128), F32)
    zero_row = jnp.zeros((C, 128), F32)
    first, last, picked, row_m, row_o = lax.fori_loop(
        0, C, gather, (zero_col, zero_col, zero_col, zero_row, zero_row)
    )
    pcol[0] = first
    pcol[1] = last
    side = jnp.where(odd == 1, last, first)
    place_m = (mine % 2) * 48 + jnp.where(is_west, 0, C)
    place_b = (beside % 2) * 48 + jnp.where(odd == 1, 0, C)
    cols_m = pltpu.roll(picked, place_m, 1)
    cols_b = pltpu.roll(side, place_b, 1)
    span_m = lane + (q_m - col0)
    span_o = lane + (q_o - col0)
    rows_m = jnp.where((span_m >= 0) & (span_m < TC), pltpu.roll(row_m, (col0 - q_m) & 127, 1), 0.0)
    rows_o = jnp.where((span_o >= 0) & (span_o < TC), pltpu.roll(row_o, (col0 - q_o) & 127, 1), 0.0)
    for t in range(G):
        a_m = jnp.where((mine // 2 == t) & (is_west | is_east), 1, 0)
        a_b = jnp.where((beside // 2 == t) & beside_on, 1, 0)
        item[t, pl.ds(0, TR), :] = jnp.where(a_m == 1, cols_m, 0.0) + jnp.where(a_b == 1, cols_b, 0.0)
        for a in range(2):
            s_m = jnp.where((mine == 2 * t + a) & (is_south | is_north), 1, 0)
            s_o = jnp.where((other == 2 * t + a) & other_on, 1, 0)
            item[t, pl.ds(TR + C * a, C), :] = jnp.where(s_m == 1, rows_m, 0.0) + jnp.where(
                s_o == 1, rows_o, 0.0
            )

    pl.semaphore_wait(barrier, G + D - 2)

    sends = []
    for k in range(1, G):
        t = (g + k) % G
        cp = remote(item.at[t], item_in.at[g], item_sem.at[0, k], item_sem.at[1, k], "grp", t)
        cp.start()
        sends.append(cp)
    up_g, dn_g = (g + 1) % G, (g + G - 1) % G
    up_d, dn_d = (d + 1) % D, (d + D - 1) % D
    halos = [
        remote(parent.at[:, pl.ds(TR - 1, 1), :], prow_in.at[0, :, pl.ds(0, 1), :], halo_sem.at[0, 0], halo_sem.at[1, 0], "grp", up_g),
        remote(parent.at[:, pl.ds(0, 1), :], prow_in.at[1, :, pl.ds(0, 1), :], halo_sem.at[0, 1], halo_sem.at[1, 1], "grp", dn_g),
        remote(pcol.at[1], pcol_in.at[0], halo_sem.at[0, 2], halo_sem.at[1, 2], "dev", up_d),
        remote(pcol.at[0], pcol_in.at[1], halo_sem.at[0, 3], halo_sem.at[1, 3], "dev", dn_d),
        remote(work.at[pl.ds(NR, 3)], work.at[pl.ds(0, 3)], halo_sem.at[0, 4], halo_sem.at[1, 4], "dev", up_d),
        remote(work.at[pl.ds(3, 3)], work.at[pl.ds(NR + 3, 3)], halo_sem.at[0, 5], halo_sem.at[1, 5], "dev", dn_d),
    ]
    for cp in halos[:4]:
        cp.start()
    for cp in own_nest:
        cp.wait()
    for cp in halos[4:]:
        cp.start()

    item_in[g] = item[g]

    for k in range(1, G):
        s = (g + G - k) % G
        remote(item.at[s], item_in.at[s], item_sem.at[0, k], item_sem.at[1, k], "grp", s).wait_recv()
    wecol[pl.ds(0, LEAD), :] = jnp.zeros((LEAD, 128), F32)
    wecol[pl.ds(LEAD + G * TR, 32), :] = jnp.zeros((32, 128), F32)
    south = [jnp.zeros((C, 128), F32)] * 2
    north = [jnp.zeros((C, 128), F32)] * 2
    r_own = [anchor[2 * g + a, 0] for a in range(2)]
    for s in range(G):
        wecol[pl.ds(LEAD + s * TR, TR), :] = item_in[s, pl.ds(0, TR), :]
        for a in range(2):
            got = item_in[s, pl.ds(TR + C * a, C), :]
            below = r_own[a] - 1 - s * TR
            above = r_own[a] + FP - s * TR
            south[a] = south[a] + jnp.where((below >= 0) & (below < TR), got, 0.0)
            north[a] = north[a] + jnp.where((above >= 0) & (above < TR), got, 0.0)
    for a in range(2):
        edge[0, pl.ds(C * a, C), :] = south[a]
        edge[1, pl.ds(C * a, C), :] = north[a]

    def strip_of(t):
        parts = [wecol[pl.ds(LEAD - 1 + r_own[a] + 8 * t, 16), :] for a in range(2)]
        return jnp.where(lane < 48, parts[0], parts[1])

    for k in range(1, D):
        t = (d + k) % D
        strip[k] = strip_of(t)
        cp = remote(strip.at[k], strip_in.at[k], strip_sem.at[0, k], strip_sem.at[1, k], "dev", t)
        cp.start()
        sends.append(cp)
    strip_in[0] = strip_of(d)

    for e, end in ((0, 0), (1, D - 1)):

        @pl.when(d != end)
        def _(e=e, end=end):
            remote(edge.at[e], edge_in.at[d], edge_sem.at[0, e], edge_sem.at[1, d], "dev", end).start()

    for cp in halos[:4]:
        cp.wait()
    tile = iota((TR, 128), 0)

    def parent_step(c, _):
        mid = pv[c]
        kx, ky = diff[0, c], diff[1, c]
        ax, ay = cour[0, c], cour[1, c]
        gw = jnp.where(d == 0, 0.0, pltpu.roll(pcol_in[0], (128 - c) & 127, 1))
        ge = jnp.where(d == D - 1, 0.0, pltpu.roll(pcol_in[1], 127 - c, 1))
        gs = jnp.where(g == 0, 0.0, prow_in[0, c, 0:1, :])
        gn = jnp.where(g == G - 1, 0.0, prow_in[1, c, 0:1, :])
        west = jnp.where(lane == 0, gw, pltpu.roll(mid, 1, 1))
        east = jnp.where(lane == 127, ge, pltpu.roll(mid, 127, 1))
        below = jnp.where(tile == 0, gs, pltpu.roll(mid, 1, 0))
        above = jnp.where(tile == TR - 1, gn, pltpu.roll(mid, TR - 1, 0))
        adv[c] = (
            mid * (1.0 - 2.0 * kx - 2.0 * ky - ax - ay)
            + kx * east
            + (kx + ax) * west
            + ky * above
            + (ky + ay) * below
        )
        return 0

    lax.fori_loop(0, C, parent_step, 0)

    for k in range(1, D):
        remote(strip.at[k], strip_in.at[k], strip_sem.at[0, k], strip_sem.at[1, k], "dev", d).wait_recv()
    total = strip_in[0]
    for k in range(1, D):
        total = total + strip_in[k]
    ghost[...] = jnp.transpose(jnp.concatenate([total, jnp.zeros((112, 128), F32)], axis=0))

    for e, end in ((0, 0), (1, D - 1)):

        @pl.when(d == end)
        def _(e=e, end=end):
            whole = edge[e]
            for k in range(1, D):
                s = (end + k) % D
                remote(edge.at[e], edge_in.at[s], edge_sem.at[0, e], edge_sem.at[1, s], "dev", end).wait_recv()
            for k in range(1, D):
                whole = whole + edge_in[(end + k) % D]
            off = iota((TC, NC), 1) - 3 * iota((TC, NC), 0)
            spread = jnp.where((off >= 0) & (off < 3), 1.0, 0.0).astype(BF16)
            fine[...] = sum(
                jnp.dot(part, spread, preferred_element_type=F32) for part in split3(whole)
            )

        @pl.when(d != end)
        def _(e=e, end=end):
            remote(edge.at[e], edge_in.at[d], edge_sem.at[0, e], edge_sem.at[1, d], "dev", end).wait_send()

    for cp in halos[4:]:
        cp.wait()

    off = iota((NC, TC), 0) - 3 * iota((NC, TC), 1)
    collect = jnp.where((off >= 0) & (off < 3), 1.0, 0.0).astype(BF16)
    first_dev, last_dev = d == 0, d == D - 1
    tiles = range(3)

    def substeps(j, a):
        plane = pl.ds(pl.multiple_of(C * a + 8 * j, 8), 8)
        k_c, k_x, k_w, k_y, k_s = (coef[i, pl.ds(8 * j, 8), :] for i in range(5))
        west = ghost[pl.ds(pl.multiple_of(48 * a + 8 * j, 8), 8), :]
        east = ghost[pl.ds(pl.multiple_of(48 * a + C + 8 * j, 8), 8), :]
        held = [fine[plane, pl.ds(128 * i, 128)] for i in tiles]
        sides = {}

        def ghosts(w):
            i = w // 3
            if i not in sides:
                sides[i] = (pltpu.roll(west, (128 - i) % 128, 1), pltpu.roll(east, 127 - i, 1))
            return sides[i]

        def keep(w, row):
            if w == 2:
                return [jnp.where(first_dev, held[i], row[i]) for i in tiles]
            if w == NR + 3:
                return [jnp.where(last_dev, held[i], row[i]) for i in tiles]
            return row

        def advance(w, below, row, above):
            gw, ge = ghosts(w)
            right = [gw] + [pltpu.roll(v, 1, 1) for v in row]
            left = [pltpu.roll(v, 127, 1) for v in row] + [ge]
            return [
                k_c * row[i]
                + k_x * jnp.where(lane == 127, left[i + 1], left[i])
                + k_w * jnp.where(lane == 0, right[i], right[i + 1])
                + k_y * above[i]
                + k_s * below[i]
                for i in tiles
            ]

        levels = [{}, {}, {}]
        acc = None
        for w in range(NR + 6):
            levels[0][w] = keep(w, [work[w, plane, pl.ds(128 * i, 128)] for i in tiles])
            for n in range(3):
                v = w - n - 1
                if v <= n or v >= NR + 5 - n:
                    continue
                src = levels[n]
                made = advance(v, src[v - 1], src[v], src[v + 1])
                del src[v - 1]
                if n < 2:
                    levels[n + 1][v] = keep(v, made)
                    continue
                for i in tiles:
                    res[v - 3, plane, pl.ds(128 * i, 128)] = made[i]
                acc = made if (v - 3) % 3 == 0 else [x + y for x, y in zip(acc, made)]
                if (v - 3) % 3 == 2:
                    at = pl.ds(pl.multiple_of(64 * a + 8 * ((v - 3) // 3), 8), 8)
                    for i in tiles:
                        triple[at, pl.ds(128 * i, 128)] = acc[i]

    pair = g + 1 - 2 * core

    def slab_copy(j, k, t, mine_g):
        return remote(
            avg.at[j, :, pl.ds(4 * (t % 2), 4)],
            slabs[j].at[pl.ds(2 * mine_g, 2)],
            slab_sem.at[0, j, k],
            slab_sem.at[1, j, k],
            "grp",
            t,
        )

    def canvas_copy(j, k, t, mine_d):
        return remote(
            slab_out.at[j, k],
            canvas[j].at[8 + mine_d, core],
            canvas_sem.at[0, j, k],
            canvas_sem.at[1, j, k],
            "dev",
            t,
        )

    def pair_copy(j, half):
        block = canvas[j].at[pl.ds(8, D), half]
        return remote(block, block, pair_sem.at[0, j], pair_sem.at[1, j], "grp", pair)

    def to_groups(j):
        for k in range(1, G):
            cp = slab_copy(j, k, (g + k) % G, g)
            cp.start()
            sends.append(cp)
        slabs[j][pl.ds(2 * g, 2)] = avg[j, :, pl.ds(4 * core, 4)]

    def to_columns(j):
        for k in range(1, G):
            slab_copy(j, k, g, (g + G - k) % G).wait_recv()
        for k in range(1, D):
            t = (d + k) % D
            slab_out[j, k] = slabs[j][tab[t // 2]]
            cp = canvas_copy(j, k, t, d)
            cp.start()
            sends.append(cp)
        canvas[j][8 + d, core] = slabs[j][mine]

    def to_pair(j):
        for k in range(1, D):
            canvas_copy(j, k, d, (d + D - k) % D).wait_recv()
        cp = pair_copy(j, core)
        cp.start()
        sends.append(cp)

    own_row = jnp.clip(row0 - r_m, -TR, FP) + TR
    shift = (q_m - col0) & 127
    tile_row = iota((TR, 128), 0) + (row0 - r_m)
    tile_col = iota((TR, 128), 1) + (col0 - q_m)
    covered = (tile_row >= 0) & (tile_row < FP) & (tile_col >= 0) & (tile_col < FP)
    rows_of = [c.reshape(256, 8, TC) for c in canvas]
    outs = []

    def place(j):
        pair_copy(j, 1 - core).wait_recv()
        window[...] = rows_of[j][pl.ds(own_row, TR)].reshape(8 * TR, TC)
        for i in range(8):
            c = 8 * j + i
            under = pltpu.roll(window[pl.ds(i, TR, stride=8), :], shift, 1)
            adv[c] = jnp.where(covered, under, adv[c])
        cp = pltpu.make_async_copy(adv.at[pl.ds(8 * j, 8)], pout.at[pl.ds(8 * j, 8)], local_sem.at[1 + j])
        cp.start()
        outs.append(cp)

    for j in range(3):

        def one(a, _, j=j):
            substeps(j, a)
            return 0

        lax.fori_loop(0, 2, one, 0)
        x = triple[...]
        hi = x.astype(BF16)
        lo = (x - hi.astype(F32)).astype(BF16)
        mean = jnp.dot(hi, collect, preferred_element_type=F32) + jnp.dot(lo, collect, preferred_element_type=F32)
        avg[j] = (mean * (1.0 / 9.0)).reshape(2, 8, 8, TC)
        to_groups(j)
    for r in range(NR):
        cp = pltpu.make_async_copy(res.at[r], nout.at[:, r, :], row_sem.at[r])
        cp.start()
        outs.append(cp)
    for j in range(3):
        to_columns(j)
    for j in range(3):
        to_pair(j)
    for j in range(3):
        place(j)
    for cp in sends:
        cp.wait_send()
    for cp in outs:
        cp.wait()


def shards(parent, nest, anchor, diffusion, courant):
    any_space = pl.BlockSpec(memory_space=pl.ANY)
    scalars = pl.BlockSpec(memory_space=pltpu.SMEM)
    dma = pltpu.SemaphoreType.DMA
    vmem = pltpu.VMEM
    pout, nout = pl.pallas_call(
        kernel,
        out_shape=(
            jax.ShapeDtypeStruct((C, TR, TC), F32),
            jax.ShapeDtypeStruct((PLANES, NR, NC), F32),
        ),
        in_specs=[scalars] * 3 + [any_space] * 2,
        out_specs=(any_space, any_space),
        scratch_shapes=[
            vmem((NR + 6, PLANES, NC), F32),
            vmem((NR, PLANES, NC), F32),
            vmem((C, TR, TC), F32),
            vmem((2, C, 8, TC), F32),
            vmem((2, TR, 128), F32),
            vmem((2, TR, 128), F32),
            vmem((G, TR + PLANES, 128), F32),
            vmem((G, TR + PLANES, 128), F32),
            vmem((LEAD + G * TR + 32, 128), F32),
            vmem((D, 16, 128), F32),
            vmem((D, 16, 128), F32),
            vmem((2, PLANES, 128), F32),
            vmem((D, PLANES, 128), F32),
            vmem((128, 128), F32),
            vmem((PLANES, NC), F32),
            vmem((5, C, 128), F32),
            vmem((128, NC), F32),
            vmem((3, 2, 8, 8, TC), F32),
            *[vmem((NESTS, 4, 8, TC), F32)] * 3,
            vmem((3, D, 4, 8, TC), F32),
            *[vmem((32, 2, 4, 8, TC), F32)] * 3,
            vmem((8 * TR, TC), F32),
            vmem((C, TR, TC), F32),
            pltpu.SMEM((8,), I32),
            dma((NR,)),
            dma((4,)),
            dma((2, 6)),
            dma((2, G)),
            dma((2, D)),
            dma((2, D)),
            dma((2, 3, G)),
            dma((2, 3, D)),
            dma((2, 3)),
        ],
        compiler_params=pltpu.CompilerParams(
            collective_id=0, has_side_effects=True, vmem_limit_bytes=48 * 1024 * 1024
        ),
    )(anchor, diffusion, courant, parent, nest.reshape(PLANES, NR, NC))
    return pout, nout.reshape(2, C, NR, NC)


def solution(mesh):
    placed = (P(None, "grp", "dev"), P("grp", None, "dev", None), P(), P(), P())
    return jax.shard_map(
        shards,
        mesh=mesh,
        in_specs=placed,
        out_specs=(P(None, "grp", "dev"), P("grp", None, "dev", None)),
        check_vma=False,
    )
```

```python
import functools

import jax
import jax.numpy as jnp
from jax import lax
from jax.experimental import pallas as pl
from jax.experimental.pallas import tpu as pltpu
from jax.sharding import PartitionSpec as P

F32 = jnp.float32
BF16 = jnp.bfloat16
I32 = jnp.int32
MESH = pl.DeviceIdType.MESH

G = 8
D = 16
C = 24
TR = 64
TC = 128
NR = 24
NC = 384
FP = 128
BAND = 256
NESTS = 16
PLANES = 2 * C
LEAD = 8


def iota(shape, axis):
    return lax.broadcasted_iota(I32, shape, axis)


def remote(src, dst, send, recv, axis, target):
    return pltpu.make_async_remote_copy(
        src_ref=src,
        dst_ref=dst,
        send_sem=send,
        recv_sem=recv,
        device_id={axis: target},
        device_id_type=MESH,
    )


def split3(a):
    hi = a.astype(BF16)
    rest = a - hi.astype(F32)
    mid = rest.astype(BF16)
    return hi, mid, (rest - mid.astype(F32)).astype(BF16)


def response(g, near, far, along):
    push = near * g
    a1 = along(None, push)
    b1 = along(a1, push)
    b2 = along(None, near * a1)
    c1 = along(b1, push + far * b2)
    c2 = along(b2, near * b1)
    c3 = along(None, near * b2)
    return c1, c2, c3


def select_dot(parts, matrix):
    return sum(jnp.dot(part, matrix, preferred_element_type=F32) for part in parts)


def one_hot(mask):
    return jnp.where(mask, 1.0, 0.0).astype(BF16)


def split2(a):
    hi = a.astype(BF16)
    return hi, (a - hi.astype(F32)).astype(BF16)


def kernel(
    anchor,
    diff,
    cour,
    parent,
    nest,
    pout,
    nout,
    work,
    res,
    pv,
    prow_in,
    pcol,
    pcol_in,
    item,
    item_in,
    wecol,
    strip,
    strip_in,
    edge,
    edge_in,
    ghost,
    fine,
    coef,
    triple,
    gcol,
    gcol_in,
    grow,
    grow_in,
    tall,
    col_fix,
    fix_w,
    fix_e,
    avg,
    slabs0,
    slabs1,
    slabs2,
    slab_out,
    canvas0,
    canvas1,
    canvas2,
    window,
    adv,
    tab,
    row_sem,
    local_sem,
    halo_sem,
    item_sem,
    strip_sem,
    edge_sem,
    slab_sem,
    canvas_sem,
    pair_sem,
):
    slabs = (slabs0, slabs1, slabs2)
    canvas = (canvas0, canvas1, canvas2)
    g = lax.axis_index("grp")
    d = lax.axis_index("dev")
    core = lax.rem(g, 2)
    row0 = g * TR
    col0 = d * TC
    lane = iota((1, 128), 1)

    own_parent = pltpu.make_async_copy(parent, pv, local_sem.at[0])
    own_parent.start()
    own_nest = [pltpu.make_async_copy(nest.at[:, r, :], work.at[3 + r], row_sem.at[r]) for r in range(NR)]
    for cp in own_nest:
        cp.start()
    barrier = pltpu.get_barrier_semaphore()
    for k in range(1, G):
        pl.semaphore_signal(barrier, inc=1, device_id={"grp": lax.rem(g + k, G)}, device_id_type=MESH)
    for k in range(1, D):
        pl.semaphore_signal(barrier, inc=1, device_id={"dev": lax.rem(d + k, D)}, device_id_type=MESH)

    for cp in own_nest:
        cp.wait()
    pl.semaphore_wait(barrier, G + D - 2)

    sends = []
    up_g, dn_g = lax.rem(g + 1, G), lax.rem(g + G - 1, G)
    up_d, dn_d = lax.rem(d + 1, D), lax.rem(d + D - 1, D)

    def halo(src, dst, i, axis, target):
        return remote(src, dst, halo_sem.at[0, i], halo_sem.at[1, i], axis, target)

    nest_halo = [
        halo(work.at[pl.ds(NR, 3)], work.at[pl.ds(0, 3)], 4, "dev", up_d),
        halo(work.at[pl.ds(3, 3)], work.at[pl.ds(NR + 3, 3)], 5, "dev", dn_d),
    ]
    parent_halo = [
        halo(parent.at[:, pl.ds(TR - 1, 1), :], prow_in.at[0, :, pl.ds(0, 1), :], 0, "grp", up_g),
        halo(parent.at[:, pl.ds(0, 1), :], prow_in.at[1, :, pl.ds(0, 1), :], 1, "grp", dn_g),
        halo(pcol.at[1], pcol_in.at[0], 2, "dev", up_d),
        halo(pcol.at[0], pcol_in.at[1], 3, "dev", dn_d),
    ]
    line_halo = [
        halo(gcol.at[pl.ds(TR - 8, 8)], gcol_in.at[0], 6, "grp", up_g),
        halo(gcol.at[pl.ds(0, 8)], gcol_in.at[1], 7, "grp", dn_g),
        halo(grow, grow_in.at[0], 8, "dev", up_d),
        halo(grow, grow_in.at[1], 9, "dev", dn_d),
    ]
    for cp in nest_halo + parent_halo[:2]:
        cp.start()

    key = [(anchor[0, n] >> 8) * 8 + (anchor[1, n] >> 8) for n in range(NESTS)]
    band_row = lax.div(g, 4)
    for b in range(8):
        found = jnp.int32(0)
        for n in range(NESTS):
            found = jnp.where(key[n] == band_row * 8 + b, n, found)
        tab[b] = found
    other = jnp.int32(0)
    for n in range(NESTS):
        other = jnp.where(key[n] == (1 - band_row) * 8 + lax.div(d, 2), n, other)
    mine = tab[lax.div(d, 2)]
    odd = lax.rem(d, 2)
    beside = tab[jnp.clip(lax.div(d, 2) - 1 + 2 * odd, 0, 7)]

    r_m, q_m = anchor[0, mine], anchor[1, mine]
    west_m = q_m - 1 - col0
    east_m = q_m + FP - col0
    is_west = (west_m >= 0) & (west_m < TC)
    is_east = (east_m >= 0) & (east_m < TC)
    pick = jnp.where(is_west, west_m, jnp.where(is_east, east_m, 0))
    q_b = anchor[1, beside]
    beside_on = jnp.where(odd == 1, q_b == col0 + TC, q_b + FP == col0)

    south_m = r_m - 1 - row0
    north_m = r_m + FP - row0
    is_south = (south_m >= 0) & (south_m < TR)
    is_north = (north_m >= 0) & (north_m < TR)
    row_pick = jnp.where(is_south, south_m, jnp.where(is_north, north_m, 0))
    r_o, q_o = anchor[0, other], anchor[1, other]
    low = band_row == 0
    other_on = jnp.where(low, r_o == row0 + TR, r_o + FP == row0)

    own_parent.wait()

    def gather(c, carry):
        first, last, picked, row_m, row_o = carry
        x = pv[c]
        here = lane == c
        first = jnp.where(here, pltpu.roll(x, c, 1), first)
        last = jnp.where(here, pltpu.roll(x, c + 1, 1), last)
        picked = jnp.where(here, pltpu.roll(x, (c - pick) & 127, 1), picked)
        sub = iota((C, 128), 0) == c
        row_m = jnp.where(sub, pv[c, pl.ds(row_pick, 1), :], row_m)
        edge_row = jnp.where(low, x[TR - 1 : TR], x[0:1])
        row_o = jnp.where(sub, edge_row, row_o)
        return first, last, picked, row_m, row_o

    zero_col = jnp.zeros((TR, 128), F32)
    zero_row = jnp.zeros((C, 128), F32)
    first, last, picked, row_m, row_o = lax.fori_loop(
        0, C, gather, (zero_col, zero_col, zero_col, zero_row, zero_row)
    )
    pcol[0] = first
    pcol[1] = last
    for cp in parent_halo[2:]:
        cp.start()
    side = jnp.where(odd == 1, last, first)
    place_m = (mine & 1) * 48 + jnp.where(is_west, 0, C)
    place_b = (beside & 1) * 48 + jnp.where(odd == 1, 0, C)
    cols_m = pltpu.roll(picked, place_m, 1)
    cols_b = pltpu.roll(side, place_b, 1)
    span_m = lane + (q_m - col0)
    span_o = lane + (q_o - col0)
    rows_m = jnp.where((span_m >= 0) & (span_m < TC), pltpu.roll(row_m, (col0 - q_m) & 127, 1), 0.0)
    rows_o = jnp.where((span_o >= 0) & (span_o < TC), pltpu.roll(row_o, (col0 - q_o) & 127, 1), 0.0)
    for t in range(G):
        a_m = jnp.where((mine >> 1 == t) & (is_west | is_east), 1, 0)
        a_b = jnp.where((beside >> 1 == t) & beside_on, 1, 0)
        item[t, pl.ds(0, TR), :] = jnp.where(a_m == 1, cols_m, 0.0) + jnp.where(a_b == 1, cols_b, 0.0)
        for a in range(2):
            s_m = jnp.where((mine == 2 * t + a) & (is_south | is_north), 1, 0)
            s_o = jnp.where((other == 2 * t + a) & other_on, 1, 0)
            item[t, pl.ds(TR + C * a, C), :] = jnp.where(s_m == 1, rows_m, 0.0) + jnp.where(
                s_o == 1, rows_o, 0.0
            )

    for k in range(1, G):
        t = lax.rem(g + k, G)
        cp = remote(item.at[t], item_in.at[g], item_sem.at[0, k], item_sem.at[1, k], "grp", t)
        cp.start()
        sends.append(cp)
    item_in[g] = item[g]

    lanes = [jnp.zeros((1, 128), F32)] * 5
    for c in range(C):
        kx, ky = 3.0 * diff[0, c], 3.0 * diff[1, c]
        ax, ay = cour[0, c], cour[1, c]
        here = (lane == c) | (lane == 32 + c)
        for i, v in enumerate((1.0 - 2.0 * kx - 2.0 * ky - ax - ay, kx, kx + ax, ky, ky + ay)):
            coef[i, pl.ds(c, 1), :] = jnp.full((1, 128), v, F32)
            lanes[i] = jnp.where(here, v, lanes[i])

    for cp in nest_halo:
        cp.wait()

    off = iota((NC, TC), 0) - 3 * iota((NC, TC), 1)
    collect = one_hot((off >= 0) & (off < 3))
    first_dev, last_dev = d == 0, d == D - 1
    tiles = range(3)

    def substeps(j, a):
        plane = pl.ds(pl.multiple_of(C * a + 8 * j, 8), 8)
        k_c, k_x, k_w, k_y, k_s = (coef[i, pl.ds(8 * j, 8), :] for i in range(5))
        def keep(w, row):
            if w == 2:
                return [jnp.where(first_dev, 0.0, row[i]) for i in tiles]
            if w == NR + 3:
                return [jnp.where(last_dev, 0.0, row[i]) for i in tiles]
            return row

        def advance(below, row, above):
            right = [0.0] + [pltpu.roll(v, 1, 1) for v in row]
            left = [pltpu.roll(v, 127, 1) for v in row] + [0.0]
            return [
                k_c * row[i]
                + k_x * jnp.where(lane == 127, left[i + 1], left[i])
                + k_w * jnp.where(lane == 0, right[i], right[i + 1])
                + k_y * above[i]
                + k_s * below[i]
                for i in tiles
            ]

        levels = [{}, {}, {}]
        acc = None
        for w in range(NR + 6):
            levels[0][w] = keep(w, [work[w, plane, pl.ds(128 * i, 128)] for i in tiles])
            for n in range(3):
                v = w - n - 1
                if v <= n or v >= NR + 5 - n:
                    continue
                src = levels[n]
                made = advance(src[v - 1], src[v], src[v + 1])
                del src[v - 1]
                if n < 2:
                    levels[n + 1][v] = keep(v, made)
                    continue
                for i in tiles:
                    res[v - 3, plane, pl.ds(128 * i, 128)] = made[i]
                acc = made if (v - 3) % 3 == 0 else [x + y for x, y in zip(acc, made)]
                if (v - 3) % 3 == 2:
                    at = pl.ds(pl.multiple_of(64 * a + 8 * ((v - 3) // 3), 8), 8)
                    for i in tiles:
                        triple[at, pl.ds(128 * i, 128)] = acc[i]

    pair = g + 1 - 2 * core

    def slab_copy(j, k, t, mine_g):
        return remote(
            avg.at[j, :, pl.ds(4 * (lax.rem(t, 2)), 4)],
            slabs[j].at[pl.ds(2 * mine_g, 2)],
            slab_sem.at[0, j, k],
            slab_sem.at[1, j, k],
            "grp",
            t,
        )

    def canvas_copy(j, k, t, mine_d):
        return remote(
            slab_out.at[j, k],
            canvas[j].at[8 + mine_d, core],
            canvas_sem.at[0, j, k],
            canvas_sem.at[1, j, k],
            "dev",
            t,
        )

    def pair_copy(j, half):
        block = canvas[j].at[pl.ds(8, D), half]
        return remote(block, block, pair_sem.at[0, j], pair_sem.at[1, j], "grp", pair)

    def to_groups(j):
        for k in range(1, G):
            cp = slab_copy(j, k, lax.rem(g + k, G), g)
            cp.start()
            sends.append(cp)
        slabs[j][pl.ds(2 * g, 2)] = avg[j, :, pl.ds(4 * core, 4)]

    def to_columns(j):
        for k in range(1, G):
            slab_copy(j, k, g, lax.rem(g + G - k, G)).wait_recv()
        for k in range(1, D):
            t = lax.rem(d + k, D)
            slab_out[j, k] = slabs[j][tab[lax.div(t, 2)]]
            cp = canvas_copy(j, k, t, d)
            cp.start()
            sends.append(cp)
        canvas[j][8 + d, core] = slabs[j][mine]

    def to_pair(j):
        for k in range(1, D):
            canvas_copy(j, k, d, lax.rem(d + D - k, D)).wait_recv()
        cp = pair_copy(j, core)
        cp.start()
        sends.append(cp)

    own_row = jnp.clip(row0 - r_m, -TR, FP) + TR
    shift = (q_m - col0) & 127
    tile_row = iota((TR, 128), 0) + (row0 - r_m)
    tile_col = iota((TR, 128), 1) + (col0 - q_m)
    covered = (tile_row >= 0) & (tile_row < FP) & (tile_col >= 0) & (tile_col < FP)
    rows_of = [c.reshape(256, 8, TC) for c in canvas]
    outs = []

    def place(j):
        pair_copy(j, 1 - core).wait_recv()
        window[...] = rows_of[j][pl.ds(own_row, TR)].reshape(8 * TR, TC)
        for i in range(8):
            c = 8 * j + i
            under = pltpu.roll(window[pl.ds(i, TR, stride=8), :], shift, 1)
            fix = col_fix[...]
            under += jnp.where(lane == at_w, pltpu.roll(fix, (at_w - c) & 127, 1), 0.0)
            under += jnp.where(lane == at_e, pltpu.roll(fix, (at_e - 32 - c) & 127, 1), 0.0)
            under += jnp.where(tile == row_at, row_fix[c : c + 1], 0.0)
            adv[c] = jnp.where(covered, under, adv[c])
        cp = pltpu.make_async_copy(adv.at[pl.ds(8 * j, 8)], pout.at[pl.ds(8 * j, 8)], local_sem.at[1 + j])
        cp.start()
        outs.append(cp)

    def compute(j):
        def one(a, _):
            substeps(j, a)
            return 0

        lax.fori_loop(0, 2, one, 0)
        mean = select_dot(split2(triple[...]), collect) * (1.0 / 9.0)
        avg[j] = mean.reshape(2, 8, 8, TC)
        to_groups(j)

    compute(0)
    compute(1)
    compute(2)
    to_columns(0)

    for k in range(1, G):
        s = lax.rem(g + G - k, G)
        remote(item.at[s], item_in.at[s], item_sem.at[0, k], item_sem.at[1, k], "grp", s).wait_recv()
    wecol[pl.ds(0, LEAD), :] = jnp.zeros((LEAD, 128), F32)
    wecol[pl.ds(LEAD + G * TR, 32), :] = jnp.zeros((32, 128), F32)
    south = [jnp.zeros((C, 128), F32)] * 2
    north = [jnp.zeros((C, 128), F32)] * 2
    r_own = [anchor[0, 2 * g + a] for a in range(2)]
    for s in range(G):
        wecol[pl.ds(LEAD + s * TR, TR), :] = item_in[s, pl.ds(0, TR), :]
        for a in range(2):
            got = item_in[s, pl.ds(TR + C * a, C), :]
            below = r_own[a] - 1 - s * TR
            above = r_own[a] + FP - s * TR
            south[a] = south[a] + jnp.where((below >= 0) & (below < TR), got, 0.0)
            north[a] = north[a] + jnp.where((above >= 0) & (above < TR), got, 0.0)
    for a in range(2):
        edge[0, pl.ds(C * a, C), :] = south[a]
        edge[1, pl.ds(C * a, C), :] = north[a]

    def strip_of(t):
        parts = [wecol[pl.ds(LEAD - 1 + r_own[a] + 8 * t, 16), :] for a in range(2)]
        return jnp.where(lane < 48, parts[0], parts[1])

    for k in range(1, D):
        t = lax.rem(d + k, D)
        strip[k] = strip_of(t)
        cp = remote(strip.at[k], strip_in.at[k], strip_sem.at[0, k], strip_sem.at[1, k], "dev", t)
        cp.start()
        sends.append(cp)
    strip_in[0] = strip_of(d)

    for e, end in ((0, 0), (1, D - 1)):

        @pl.when(d != end)
        def _(e=e, end=end):
            remote(edge.at[e], edge_in.at[d], edge_sem.at[0, e], edge_sem.at[1, d], "dev", end).start()

    to_columns(1)

    for cp in parent_halo:
        cp.wait()
    at_w, at_e = q_m - col0, q_m + FP - 1 - col0
    at_s, at_n = r_m - row0, r_m + FP - 1 - row0
    from_w = jnp.where(d == 0, 0.0, pcol_in[0])
    from_e = jnp.where(d == D - 1, 0.0, pcol_in[1])
    line_w = jnp.where(at_w == 0, from_w, picked)
    line_e = jnp.where(at_e == TC - 1, from_e, picked)
    gcol[...] = jnp.where(lane < 32, line_w, pltpu.roll(line_e, 32, 1))
    has_s = (at_s >= 0) & (at_s < TR)
    from_s = jnp.where(g == 0, 0.0, prow_in[0, :, 0, :])
    from_n = jnp.where(g == G - 1, 0.0, prow_in[1, :, 0, :])
    grow[...] = jnp.where(at_s == 0, from_s, jnp.where(at_n == TR - 1, from_n, row_m))
    for cp in line_halo:
        cp.start()
    to_columns(2)

    tile = iota((TR, 128), 0)

    def parent_step(c, _):
        mid = pv[c]
        kx, ky = diff[0, c], diff[1, c]
        ax, ay = cour[0, c], cour[1, c]
        gw = jnp.where(d == 0, 0.0, pltpu.roll(pcol_in[0], (128 - c) & 127, 1))
        ge = jnp.where(d == D - 1, 0.0, pltpu.roll(pcol_in[1], 127 - c, 1))
        gs = jnp.where(g == 0, 0.0, prow_in[0, c, 0:1, :])
        gn = jnp.where(g == G - 1, 0.0, prow_in[1, c, 0:1, :])
        west = jnp.where(lane == 0, gw, pltpu.roll(mid, 1, 1))
        east = jnp.where(lane == 127, ge, pltpu.roll(mid, 127, 1))
        below = jnp.where(tile == 0, gs, pltpu.roll(mid, 1, 0))
        above = jnp.where(tile == TR - 1, gn, pltpu.roll(mid, TR - 1, 0))
        adv[c] = (
            mid * (1.0 - 2.0 * kx - 2.0 * ky - ax - ay)
            + kx * east
            + (kx + ax) * west
            + ky * above
            + (ky + ay) * below
        )
        return 0

    lax.fori_loop(0, C, parent_step, 0)


    for cp in line_halo:
        cp.wait()
    column = jnp.concatenate([gcol_in[0], gcol[...], gcol_in[1]], axis=0)
    for k in range(3):
        tall[pl.ds(k, TR + 16, stride=3), :] = column
    tall_row = iota((3 * (TR + 16), 128), 0) + 3 * (row0 - r_m - 8)
    inside = (tall_row >= 0) & (tall_row < NC)
    l_c, l_x, l_w, l_y, l_s = lanes
    size = 3 * (TR + 16)

    def down(u, add):
        if u is not None:
            add += l_c * u + l_y * pltpu.roll(u, size - 1, 0) + l_s * pltpu.roll(u, 1, 0)
        return jnp.where(inside, add, 0.0)

    w_lane = lane < 32
    tall[...] = sum(response(tall[...], jnp.where(w_lane, l_w, l_x), jnp.where(w_lane, l_x, l_w), down))
    col_fix[...] = sum(tall[pl.ds(24 + k, TR, stride=3), :] for k in range(3)) * (1.0 / 9.0)

    wide = 512
    wide_off = iota((TC, wide), 1) - 64 - 3 * iota((TC, wide), 0)
    to_wide = [one_hot((wide_off + o >= 0) & (wide_off + o < 3)) for o in (NC, 0, -NC)]
    row = sum(
        select_dot(split3(v), m) for v, m in zip((grow_in[0], grow[...], grow_in[1]), to_wide)
    )
    wide_col = iota((C, wide), 1) - 64 + 3 * (col0 - q_m)
    within = (wide_col >= 0) & (wide_col < NC)
    c_c, c_x, c_w, c_y, c_s = (jnp.concatenate([coef[i]] * 4, axis=1) for i in range(5))

    def across(u, add):
        if u is not None:
            add += c_c * u + c_x * pltpu.roll(u, wide - 1, 1) + c_w * pltpu.roll(u, 1, 1)
        return jnp.where(within, add, 0.0)

    strip_sum = sum(response(row, jnp.where(has_s, c_s, c_y), jnp.where(has_s, c_y, c_s), across))
    back = iota((wide, TC), 0) - 64 - 3 * iota((wide, TC), 1)
    row_fix = select_dot(split2(strip_sum), one_hot((back >= 0) & (back < 3))) * (1.0 / 9.0)
    row_at = jnp.where(has_s, at_s, at_n)

    to_pair(0)

    for k in range(1, D):
        remote(strip.at[k], strip_in.at[k], strip_sem.at[0, k], strip_sem.at[1, k], "dev", d).wait_recv()
    total = strip_in[0]
    for k in range(1, D):
        total = total + strip_in[k]
    ghost[...] = jnp.transpose(jnp.concatenate([total, jnp.zeros((112, 128), F32)], axis=0))

    spread_off = iota((128, 128), 1) - 3 * iota((128, 128), 0)
    fine_ghost = select_dot(split3(ghost[...]), one_hot((spread_off >= 0) & (spread_off < 3)))
    open_rows = ((lane >= 3) | (d != 0)) & ((lane < NR + 3) | (d != D - 1)) & (lane < NR + 6)
    n_c, n_x, n_w, n_y, n_s = (jnp.concatenate([coef[i]] * 2, axis=0) for i in range(5))

    def along(u, add):
        if u is not None:
            add += n_c * u + n_y * pltpu.roll(u, 127, 1) + n_s * pltpu.roll(u, 1, 1)
        return jnp.where(open_rows, add, 0.0)

    pack_off = iota((128, 128), 1) - 3 * (iota((128, 128), 0) - 3)
    packed = []
    for side, near, far in ((0, n_w, n_x), (1, n_x, n_w)):
        g_side = jnp.concatenate([fine_ghost[48 * a + C * side : 48 * a + C * side + C] for a in range(2)], axis=0)
        lines = response(g_side, near, far, along)
        packed.append(
            sum(
                select_dot(split2(v), one_hot(pack_off == (k if side == 0 else 2 - k)))
                for k, v in enumerate(lines)
            )
        )
    fix_w[...] = packed[0]
    fix_e[...] = packed[1]

    def fix_cols(t, _):
        plane = pl.ds(pl.multiple_of(8 * t, 8), 8)
        w_fix, e_fix = fix_w[plane, :], fix_e[plane, :]
        for f in range(NR):
            res[f, plane, pl.ds(0, 128)] += jnp.where(lane < 3, pltpu.roll(w_fix, (128 - 3 * f) % 128, 1), 0.0)
            res[f, plane, pl.ds(256, 128)] += jnp.where(lane >= 125, pltpu.roll(e_fix, (125 - 3 * f) % 128, 1), 0.0)
        return 0

    lax.fori_loop(0, 6, fix_cols, 0)

    def store_rows(some):
        for r in some:
            cp = pltpu.make_async_copy(res.at[r], nout.at[:, r, :], row_sem.at[r])
            cp.start()
            outs.append(cp)

    store_rows(range(3, NR - 3))
    to_pair(1)
    to_pair(2)
    place(0)

    for e, end in ((0, 0), (1, D - 1)):

        @pl.when(d == end)
        def _(e=e, end=end):
            whole = edge[e]
            for k in range(1, D):
                s = (end + k) % D
                remote(edge.at[e], edge_in.at[s], edge_sem.at[0, e], edge_sem.at[1, s], "dev", end).wait_recv()
            for k in range(1, D):
                whole = whole + edge_in[(end + k) % D]
            off = iota((TC, NC), 1) - 3 * iota((TC, NC), 0)
            spread = jnp.where((off >= 0) & (off < 3), 1.0, 0.0).astype(BF16)
            fine[...] = sum(
                jnp.dot(part, spread, preferred_element_type=F32) for part in split3(whole)
            )

        @pl.when(d != end)
        def _(e=e, end=end):
            remote(edge.at[e], edge_in.at[d], edge_sem.at[0, e], edge_sem.at[1, d], "dev", end).wait_send()


    for e, end in ((0, 0), (1, D - 1)):

        @pl.when(d == end)
        def _(e=e):
            n3 = [jnp.concatenate([v] * 3, axis=1) for v in (n_c, n_x, n_w, n_y, n_s)]
            at = iota((PLANES, NC), 1)

            def over(u, add):
                if u is None:
                    return add
                right = jnp.where(at == NC - 1, 0.0, pltpu.roll(u, NC - 1, 1))
                left = jnp.where(at == 0, 0.0, pltpu.roll(u, 1, 1))
                return n3[0] * u + n3[1] * right + n3[2] * left + add

            near, far = (n3[4], n3[3]) if e == 0 else (n3[3], n3[4])
            for k, v in enumerate(response(fine[...], near, far, over)):
                res[k if e == 0 else NR - 1 - k] += v

    store_rows([0, 1, 2, NR - 3, NR - 2, NR - 1])
    place(1)
    place(2)
    for cp in sends:
        cp.wait_send()
    for cp in outs:
        cp.wait()


def shards(parent, nest, anchor, diffusion, courant):
    any_space = pl.BlockSpec(memory_space=pl.ANY)
    scalars = pl.BlockSpec(memory_space=pltpu.SMEM)
    dma = pltpu.SemaphoreType.DMA
    vmem = pltpu.VMEM
    pout, nout = pl.pallas_call(
        kernel,
        out_shape=(
            jax.ShapeDtypeStruct((C, TR, TC), F32),
            jax.ShapeDtypeStruct((PLANES, NR, NC), F32),
        ),
        in_specs=[scalars] * 3 + [any_space] * 2,
        out_specs=(any_space, any_space),
        scratch_shapes=[
            vmem((NR + 6, PLANES, NC), F32),
            vmem((NR, PLANES, NC), F32),
            vmem((C, TR, TC), F32),
            vmem((2, C, 8, TC), F32),
            vmem((2, TR, 128), F32),
            vmem((2, TR, 128), F32),
            vmem((G, TR + PLANES, 128), F32),
            vmem((G, TR + PLANES, 128), F32),
            vmem((LEAD + G * TR + 32, 128), F32),
            vmem((D, 16, 128), F32),
            vmem((D, 16, 128), F32),
            vmem((2, PLANES, 128), F32),
            vmem((D, PLANES, 128), F32),
            vmem((128, 128), F32),
            vmem((PLANES, NC), F32),
            vmem((5, C, 128), F32),
            vmem((128, NC), F32),
            vmem((TR, 128), F32),
            vmem((2, 8, 128), F32),
            vmem((C, 128), F32),
            vmem((2, C, 128), F32),
            vmem((3 * (TR + 16), 128), F32),
            vmem((TR, 128), F32),
            vmem((PLANES, 128), F32),
            vmem((PLANES, 128), F32),
            vmem((3, 2, 8, 8, TC), F32),
            *[vmem((NESTS, 4, 8, TC), F32)] * 3,
            vmem((3, D, 4, 8, TC), F32),
            *[vmem((32, 2, 4, 8, TC), F32)] * 3,
            vmem((8 * TR, TC), F32),
            vmem((C, TR, TC), F32),
            pltpu.SMEM((8,), I32),
            dma((NR,)),
            dma((4,)),
            dma((2, 10)),
            dma((2, G)),
            dma((2, D)),
            dma((2, D)),
            dma((2, 3, G)),
            dma((2, 3, D)),
            dma((2, 3)),
        ],
        compiler_params=pltpu.CompilerParams(
            collective_id=0, has_side_effects=True, vmem_limit_bytes=60 * 1024 * 1024
        ),
    )(anchor.T, diffusion, courant, parent, nest.reshape(PLANES, NR, NC))
    return pout, nout.reshape(2, C, NR, NC)


def solution(mesh):
    placed = (P(None, "grp", "dev"), P("grp", None, "dev", None), P(), P(), P())
    return jax.shard_map(
        shards,
        mesh=mesh,
        in_specs=placed,
        out_specs=(P(None, "grp", "dev"), P("grp", None, "dev", None)),
        check_vma=False,
    )
```

```python
import functools

import jax
import jax.numpy as jnp
from jax import lax
from jax.experimental import pallas as pl
from jax.experimental.pallas import tpu as pltpu
from jax.sharding import PartitionSpec as P

F32 = jnp.float32
BF16 = jnp.bfloat16
I32 = jnp.int32
MESH = pl.DeviceIdType.MESH

G = 8
D = 16
C = 24
TR = 64
TC = 128
NR = 24
NC = 384
FP = 128
BAND = 256
NESTS = 16
PLANES = 2 * C
LEAD = 8


def iota(shape, axis):
    return lax.broadcasted_iota(I32, shape, axis)


def remote(src, dst, send, recv, axis, target):
    return pltpu.make_async_remote_copy(
        src_ref=src,
        dst_ref=dst,
        send_sem=send,
        recv_sem=recv,
        device_id={axis: target},
        device_id_type=MESH,
    )


def split3(a):
    hi = a.astype(BF16)
    rest = a - hi.astype(F32)
    mid = rest.astype(BF16)
    return hi, mid, (rest - mid.astype(F32)).astype(BF16)


def response(g, near, far, along):
    push = near * g
    a1 = along(None, push)
    b1 = along(a1, push)
    b2 = along(None, near * a1)
    c1 = along(b1, push + far * b2)
    c2 = along(b2, near * b1)
    c3 = along(None, near * b2)
    return c1, c2, c3


def select_dot(parts, matrix):
    return sum(jnp.dot(part, matrix, preferred_element_type=F32) for part in parts)


def one_hot(mask):
    return jnp.where(mask, 1.0, 0.0).astype(BF16)


def split2(a):
    hi = a.astype(BF16)
    return hi, (a - hi.astype(F32)).astype(BF16)


def kernel(
    anchor,
    diff,
    cour,
    parent,
    nest,
    pout,
    nout,
    work,
    res,
    pv,
    prow_in,
    pcol,
    pcol_in,
    item,
    item_in,
    wecol,
    strip,
    strip_in,
    edge,
    edge_in,
    ghost,
    fine,
    coef,
    triple,
    gcol,
    gcol_in,
    grow,
    grow_in,
    tall,
    col_fix,
    fix_w,
    fix_e,
    avg,
    slabs0,
    slabs1,
    slabs2,
    slab_out,
    canvas0,
    canvas1,
    canvas2,
    window,
    adv,
    tab,
    row_sem,
    local_sem,
    halo_sem,
    item_sem,
    strip_sem,
    edge_sem,
    slab_sem,
    canvas_sem,
    pair_sem,
):
    slabs = (slabs0, slabs1, slabs2)
    canvas = (canvas0, canvas1, canvas2)
    g = lax.axis_index("grp")
    d = lax.axis_index("dev")
    core = lax.rem(g, 2)
    row0 = g * TR
    col0 = d * TC
    lane = iota((1, 128), 1)

    own_parent = pltpu.make_async_copy(parent, pv, local_sem.at[0])
    own_parent.start()
    own_nest = [pltpu.make_async_copy(nest.at[:, r, :], work.at[3 + r], row_sem.at[r]) for r in range(NR)]
    for cp in own_nest:
        cp.start()
    barrier = pltpu.get_barrier_semaphore()
    for k in range(1, G):
        pl.semaphore_signal(barrier, inc=1, device_id={"grp": lax.rem(g + k, G)}, device_id_type=MESH)
    for k in range(1, D):
        pl.semaphore_signal(barrier, inc=1, device_id={"dev": lax.rem(d + k, D)}, device_id_type=MESH)

    for cp in own_nest:
        cp.wait()
    pl.semaphore_wait(barrier, G + D - 2)

    sends = []
    up_g, dn_g = lax.rem(g + 1, G), lax.rem(g + G - 1, G)
    up_d, dn_d = lax.rem(d + 1, D), lax.rem(d + D - 1, D)

    def halo(src, dst, i, axis, target):
        return remote(src, dst, halo_sem.at[0, i], halo_sem.at[1, i], axis, target)

    nest_halo = [
        halo(work.at[pl.ds(NR, 3)], work.at[pl.ds(0, 3)], 4, "dev", up_d),
        halo(work.at[pl.ds(3, 3)], work.at[pl.ds(NR + 3, 3)], 5, "dev", dn_d),
    ]
    parent_halo = [
        halo(parent.at[:, pl.ds(TR - 1, 1), :], prow_in.at[0, :, pl.ds(0, 1), :], 0, "grp", up_g),
        halo(parent.at[:, pl.ds(0, 1), :], prow_in.at[1, :, pl.ds(0, 1), :], 1, "grp", dn_g),
        halo(pcol.at[1], pcol_in.at[0], 2, "dev", up_d),
        halo(pcol.at[0], pcol_in.at[1], 3, "dev", dn_d),
    ]
    line_halo = [
        halo(gcol.at[pl.ds(TR - 8, 8)], gcol_in.at[0], 6, "grp", up_g),
        halo(gcol.at[pl.ds(0, 8)], gcol_in.at[1], 7, "grp", dn_g),
        halo(grow, grow_in.at[0], 8, "dev", up_d),
        halo(grow, grow_in.at[1], 9, "dev", dn_d),
    ]
    for cp in nest_halo + parent_halo[:2]:
        cp.start()

    key = [(anchor[0, n] >> 8) * 8 + (anchor[1, n] >> 8) for n in range(NESTS)]
    band_row = lax.div(g, 4)
    for b in range(8):
        found = jnp.int32(0)
        for n in range(NESTS):
            found = jnp.where(key[n] == band_row * 8 + b, n, found)
        tab[b] = found
    other = jnp.int32(0)
    for n in range(NESTS):
        other = jnp.where(key[n] == (1 - band_row) * 8 + lax.div(d, 2), n, other)
    mine = tab[lax.div(d, 2)]
    odd = lax.rem(d, 2)
    beside = tab[jnp.clip(lax.div(d, 2) - 1 + 2 * odd, 0, 7)]

    r_m, q_m = anchor[0, mine], anchor[1, mine]
    west_m = q_m - 1 - col0
    east_m = q_m + FP - col0
    is_west = (west_m >= 0) & (west_m < TC)
    is_east = (east_m >= 0) & (east_m < TC)
    pick = jnp.where(is_west, west_m, jnp.where(is_east, east_m, 0))
    q_b = anchor[1, beside]
    beside_on = jnp.where(odd == 1, q_b == col0 + TC, q_b + FP == col0)

    south_m = r_m - 1 - row0
    north_m = r_m + FP - row0
    is_south = (south_m >= 0) & (south_m < TR)
    is_north = (north_m >= 0) & (north_m < TR)
    row_pick = jnp.where(is_south, south_m, jnp.where(is_north, north_m, 0))
    r_o, q_o = anchor[0, other], anchor[1, other]
    low = band_row == 0
    other_on = jnp.where(low, r_o == row0 + TR, r_o + FP == row0)

    own_parent.wait()

    def gather(c, carry):
        first, last, picked, row_m, row_o = carry
        x = pv[c]
        here = lane == c
        first = jnp.where(here, pltpu.roll(x, c, 1), first)
        last = jnp.where(here, pltpu.roll(x, c + 1, 1), last)
        picked = jnp.where(here, pltpu.roll(x, (c - pick) & 127, 1), picked)
        sub = iota((C, 128), 0) == c
        row_m = jnp.where(sub, pv[c, pl.ds(row_pick, 1), :], row_m)
        edge_row = jnp.where(low, x[TR - 1 : TR], x[0:1])
        row_o = jnp.where(sub, edge_row, row_o)
        return first, last, picked, row_m, row_o

    zero_col = jnp.zeros((TR, 128), F32)
    zero_row = jnp.zeros((C, 128), F32)
    first, last, picked, row_m, row_o = lax.fori_loop(
        0, C, gather, (zero_col, zero_col, zero_col, zero_row, zero_row)
    )
    pcol[0] = first
    pcol[1] = last
    for cp in parent_halo[2:]:
        cp.start()
    side = jnp.where(odd == 1, last, first)
    place_m = (mine & 1) * 48 + jnp.where(is_west, 0, C)
    place_b = (beside & 1) * 48 + jnp.where(odd == 1, 0, C)
    cols_m = pltpu.roll(picked, place_m, 1)
    cols_b = pltpu.roll(side, place_b, 1)
    span_m = lane + (q_m - col0)
    span_o = lane + (q_o - col0)
    rows_m = jnp.where((span_m >= 0) & (span_m < TC), pltpu.roll(row_m, (col0 - q_m) & 127, 1), 0.0)
    rows_o = jnp.where((span_o >= 0) & (span_o < TC), pltpu.roll(row_o, (col0 - q_o) & 127, 1), 0.0)
    for t in range(G):
        a_m = jnp.where((mine >> 1 == t) & (is_west | is_east), 1, 0)
        a_b = jnp.where((beside >> 1 == t) & beside_on, 1, 0)
        item[t, pl.ds(0, TR), :] = jnp.where(a_m == 1, cols_m, 0.0) + jnp.where(a_b == 1, cols_b, 0.0)
        for a in range(2):
            s_m = jnp.where((mine == 2 * t + a) & (is_south | is_north), 1, 0)
            s_o = jnp.where((other == 2 * t + a) & other_on, 1, 0)
            item[t, pl.ds(TR + C * a, C), :] = jnp.where(s_m == 1, rows_m, 0.0) + jnp.where(
                s_o == 1, rows_o, 0.0
            )

    for k in range(1, G):
        t = lax.rem(g + k, G)
        cp = remote(item.at[t], item_in.at[g], item_sem.at[0, k], item_sem.at[1, k], "grp", t)
        cp.start()
        sends.append(cp)
    item_in[g] = item[g]

    lanes = [jnp.zeros((1, 128), F32)] * 5
    for c in range(C):
        kx, ky = 3.0 * diff[0, c], 3.0 * diff[1, c]
        ax, ay = cour[0, c], cour[1, c]
        here = (lane == c) | (lane == 32 + c)
        for i, v in enumerate((1.0 - 2.0 * kx - 2.0 * ky - ax - ay, kx, kx + ax, ky, ky + ay)):
            coef[i, pl.ds(c, 1), :] = jnp.full((1, 128), v, F32)
            lanes[i] = jnp.where(here, v, lanes[i])

    for cp in nest_halo:
        cp.wait()

    off = iota((NC, TC), 0) - 3 * iota((NC, TC), 1)
    collect = one_hot((off >= 0) & (off < 3))
    first_dev, last_dev = d == 0, d == D - 1
    tiles = range(3)

    def substeps(j, a):
        plane = pl.ds(pl.multiple_of(C * a + 8 * j, 8), 8)
        k_c, k_x, k_w, k_y, k_s = (coef[i, pl.ds(8 * j, 8), :] for i in range(5))
        def keep(w, row):
            if w == 2:
                return [jnp.where(first_dev, 0.0, row[i]) for i in tiles]
            if w == NR + 3:
                return [jnp.where(last_dev, 0.0, row[i]) for i in tiles]
            return row

        def advance(below, row, above):
            right = [0.0] + [pltpu.roll(v, 1, 1) for v in row]
            left = [pltpu.roll(v, 127, 1) for v in row] + [0.0]
            return [
                k_c * row[i]
                + k_x * jnp.where(lane == 127, left[i + 1], left[i])
                + k_w * jnp.where(lane == 0, right[i], right[i + 1])
                + k_y * above[i]
                + k_s * below[i]
                for i in tiles
            ]

        levels = [{}, {}, {}]
        acc = None
        for w in range(NR + 6):
            levels[0][w] = keep(w, [work[w, plane, pl.ds(128 * i, 128)] for i in tiles])
            for n in range(3):
                v = w - n - 1
                if v <= n or v >= NR + 5 - n:
                    continue
                src = levels[n]
                made = advance(src[v - 1], src[v], src[v + 1])
                del src[v - 1]
                if n < 2:
                    levels[n + 1][v] = keep(v, made)
                    continue
                for i in tiles:
                    res[v - 3, plane, pl.ds(128 * i, 128)] = made[i]
                acc = made if (v - 3) % 3 == 0 else [x + y for x, y in zip(acc, made)]
                if (v - 3) % 3 == 2:
                    at = pl.ds(pl.multiple_of(64 * a + 8 * ((v - 3) // 3), 8), 8)
                    for i in tiles:
                        triple[at, pl.ds(128 * i, 128)] = acc[i]

    pair = g + 1 - 2 * core

    def slab_copy(j, k, t, mine_g):
        return remote(
            avg.at[j, :, pl.ds(4 * (lax.rem(t, 2)), 4)],
            slabs[j].at[pl.ds(2 * mine_g, 2)],
            slab_sem.at[0, j, k],
            slab_sem.at[1, j, k],
            "grp",
            t,
        )

    def canvas_copy(j, k, t, mine_d):
        return remote(
            slab_out.at[j, k],
            canvas[j].at[8 + mine_d, core],
            canvas_sem.at[0, j, k],
            canvas_sem.at[1, j, k],
            "dev",
            t,
        )

    def pair_copy(j, half):
        block = canvas[j].at[pl.ds(8, D), half]
        return remote(block, block, pair_sem.at[0, j], pair_sem.at[1, j], "grp", pair)

    def to_groups(j):
        for k in range(1, G):
            cp = slab_copy(j, k, lax.rem(g + k, G), g)
            cp.start()
            sends.append(cp)
        slabs[j][pl.ds(2 * g, 2)] = avg[j, :, pl.ds(4 * core, 4)]

    def to_columns(j):
        for k in range(1, G):
            slab_copy(j, k, g, lax.rem(g + G - k, G)).wait_recv()
        for k in range(1, D):
            t = lax.rem(d + k, D)
            slab_out[j, k] = slabs[j][tab[lax.div(t, 2)]]
            cp = canvas_copy(j, k, t, d)
            cp.start()
            sends.append(cp)
        canvas[j][8 + d, core] = slabs[j][mine]

    def to_pair(j):
        for k in range(1, D):
            canvas_copy(j, k, d, lax.rem(d + D - k, D)).wait_recv()
        cp = pair_copy(j, core)
        cp.start()
        sends.append(cp)

    own_row = jnp.clip(row0 - r_m, -TR, FP) + TR
    shift = (q_m - col0) & 127
    tile_row = iota((TR, 128), 0) + (row0 - r_m)
    tile_col = iota((TR, 128), 1) + (col0 - q_m)
    covered = (tile_row >= 0) & (tile_row < FP) & (tile_col >= 0) & (tile_col < FP)
    rows_of = [c.reshape(256, 8, TC) for c in canvas]
    outs = []

    def place(j):
        pair_copy(j, 1 - core).wait_recv()
        window[...] = rows_of[j][pl.ds(own_row, TR)].reshape(8 * TR, TC)
        for i in range(8):
            c = 8 * j + i
            under = pltpu.roll(window[pl.ds(i, TR, stride=8), :], shift, 1)
            fix = col_fix[...]
            under += jnp.where(lane == at_w, pltpu.roll(fix, (at_w - c) & 127, 1), 0.0)
            under += jnp.where(lane == at_e, pltpu.roll(fix, (at_e - 32 - c) & 127, 1), 0.0)
            under += jnp.where(tile == row_at, row_fix[c : c + 1], 0.0)
            adv[c] = jnp.where(covered, under, adv[c])
        cp = pltpu.make_async_copy(adv.at[pl.ds(8 * j, 8)], pout.at[pl.ds(8 * j, 8)], local_sem.at[1 + j])
        cp.start()
        outs.append(cp)

    def compute(j):
        def one(a, _):
            substeps(j, a)
            return 0

        lax.fori_loop(0, 2, one, 0)
        mean = select_dot(split2(triple[...]), collect) * (1.0 / 9.0)
        avg[j] = mean.reshape(2, 8, 8, TC)
        to_groups(j)

    compute(0)

    compute(1)

    for k in range(1, G):
        s = lax.rem(g + G - k, G)
        remote(item.at[s], item_in.at[s], item_sem.at[0, k], item_sem.at[1, k], "grp", s).wait_recv()
    wecol[pl.ds(0, LEAD), :] = jnp.zeros((LEAD, 128), F32)
    wecol[pl.ds(LEAD + G * TR, 32), :] = jnp.zeros((32, 128), F32)
    south = [jnp.zeros((C, 128), F32)] * 2
    north = [jnp.zeros((C, 128), F32)] * 2
    r_own = [anchor[0, 2 * g + a] for a in range(2)]
    for s in range(G):
        wecol[pl.ds(LEAD + s * TR, TR), :] = item_in[s, pl.ds(0, TR), :]
        for a in range(2):
            got = item_in[s, pl.ds(TR + C * a, C), :]
            below = r_own[a] - 1 - s * TR
            above = r_own[a] + FP - s * TR
            south[a] = south[a] + jnp.where((below >= 0) & (below < TR), got, 0.0)
            north[a] = north[a] + jnp.where((above >= 0) & (above < TR), got, 0.0)
    for a in range(2):
        edge[0, pl.ds(C * a, C), :] = south[a]
        edge[1, pl.ds(C * a, C), :] = north[a]

    def strip_of(t):
        parts = [wecol[pl.ds(LEAD - 1 + r_own[a] + 8 * t, 16), :] for a in range(2)]
        return jnp.where(lane < 48, parts[0], parts[1])

    for k in range(1, D):
        t = lax.rem(d + k, D)
        strip[k] = strip_of(t)
        cp = remote(strip.at[k], strip_in.at[k], strip_sem.at[0, k], strip_sem.at[1, k], "dev", t)
        cp.start()
        sends.append(cp)
    strip_in[0] = strip_of(d)

    for e, end in ((0, 0), (1, D - 1)):

        @pl.when(d != end)
        def _(e=e, end=end):
            remote(edge.at[e], edge_in.at[d], edge_sem.at[0, e], edge_sem.at[1, d], "dev", end).start()


    compute(2)

    for cp in parent_halo:
        cp.wait()
    at_w, at_e = q_m - col0, q_m + FP - 1 - col0
    at_s, at_n = r_m - row0, r_m + FP - 1 - row0
    from_w = jnp.where(d == 0, 0.0, pcol_in[0])
    from_e = jnp.where(d == D - 1, 0.0, pcol_in[1])
    line_w = jnp.where(at_w == 0, from_w, picked)
    line_e = jnp.where(at_e == TC - 1, from_e, picked)
    gcol[...] = jnp.where(lane < 32, line_w, pltpu.roll(line_e, 32, 1))
    has_s = (at_s >= 0) & (at_s < TR)
    from_s = jnp.where(g == 0, 0.0, prow_in[0, :, 0, :])
    from_n = jnp.where(g == G - 1, 0.0, prow_in[1, :, 0, :])
    grow[...] = jnp.where(at_s == 0, from_s, jnp.where(at_n == TR - 1, from_n, row_m))
    for cp in line_halo:
        cp.start()

    to_columns(0)

    to_columns(1)

    to_columns(2)

    tile = iota((TR, 128), 0)

    def parent_step(c, _):
        mid = pv[c]
        kx, ky = diff[0, c], diff[1, c]
        ax, ay = cour[0, c], cour[1, c]
        gw = jnp.where(d == 0, 0.0, pltpu.roll(pcol_in[0], (128 - c) & 127, 1))
        ge = jnp.where(d == D - 1, 0.0, pltpu.roll(pcol_in[1], 127 - c, 1))
        gs = jnp.where(g == 0, 0.0, prow_in[0, c, 0:1, :])
        gn = jnp.where(g == G - 1, 0.0, prow_in[1, c, 0:1, :])
        west = jnp.where(lane == 0, gw, pltpu.roll(mid, 1, 1))
        east = jnp.where(lane == 127, ge, pltpu.roll(mid, 127, 1))
        below = jnp.where(tile == 0, gs, pltpu.roll(mid, 1, 0))
        above = jnp.where(tile == TR - 1, gn, pltpu.roll(mid, TR - 1, 0))
        adv[c] = (
            mid * (1.0 - 2.0 * kx - 2.0 * ky - ax - ay)
            + kx * east
            + (kx + ax) * west
            + ky * above
            + (ky + ay) * below
        )
        return 0

    lax.fori_loop(0, C, parent_step, 0)


    for cp in line_halo:
        cp.wait()
    column = jnp.concatenate([gcol_in[0], gcol[...], gcol_in[1]], axis=0)
    for k in range(3):
        tall[pl.ds(k, TR + 16, stride=3), :] = column
    tall_row = iota((3 * (TR + 16), 128), 0) + 3 * (row0 - r_m - 8)
    inside = (tall_row >= 0) & (tall_row < NC)
    l_c, l_x, l_w, l_y, l_s = lanes
    size = 3 * (TR + 16)

    def down(u, add):
        if u is not None:
            add += l_c * u + l_y * pltpu.roll(u, size - 1, 0) + l_s * pltpu.roll(u, 1, 0)
        return jnp.where(inside, add, 0.0)

    w_lane = lane < 32
    tall[...] = sum(response(tall[...], jnp.where(w_lane, l_w, l_x), jnp.where(w_lane, l_x, l_w), down))
    col_fix[...] = sum(tall[pl.ds(24 + k, TR, stride=3), :] for k in range(3)) * (1.0 / 9.0)

    wide = 512
    wide_off = iota((TC, wide), 1) - 64 - 3 * iota((TC, wide), 0)
    to_wide = [one_hot((wide_off + o >= 0) & (wide_off + o < 3)) for o in (NC, 0, -NC)]
    row = sum(
        select_dot(split3(v), m) for v, m in zip((grow_in[0], grow[...], grow_in[1]), to_wide)
    )
    wide_col = iota((C, wide), 1) - 64 + 3 * (col0 - q_m)
    within = (wide_col >= 0) & (wide_col < NC)
    c_c, c_x, c_w, c_y, c_s = (jnp.concatenate([coef[i]] * 4, axis=1) for i in range(5))

    def across(u, add):
        if u is not None:
            add += c_c * u + c_x * pltpu.roll(u, wide - 1, 1) + c_w * pltpu.roll(u, 1, 1)
        return jnp.where(within, add, 0.0)

    strip_sum = sum(response(row, jnp.where(has_s, c_s, c_y), jnp.where(has_s, c_y, c_s), across))
    back = iota((wide, TC), 0) - 64 - 3 * iota((wide, TC), 1)
    row_fix = select_dot(split2(strip_sum), one_hot((back >= 0) & (back < 3))) * (1.0 / 9.0)
    row_at = jnp.where(has_s, at_s, at_n)

    to_pair(0)

    for k in range(1, D):
        remote(strip.at[k], strip_in.at[k], strip_sem.at[0, k], strip_sem.at[1, k], "dev", d).wait_recv()
    total = strip_in[0]
    for k in range(1, D):
        total = total + strip_in[k]
    ghost[...] = jnp.transpose(jnp.concatenate([total, jnp.zeros((112, 128), F32)], axis=0))

    spread_off = iota((128, 128), 1) - 3 * iota((128, 128), 0)
    fine_ghost = select_dot(split3(ghost[...]), one_hot((spread_off >= 0) & (spread_off < 3)))
    open_rows = ((lane >= 3) | (d != 0)) & ((lane < NR + 3) | (d != D - 1)) & (lane < NR + 6)
    n_c, n_x, n_w, n_y, n_s = (jnp.concatenate([coef[i]] * 2, axis=0) for i in range(5))

    def along(u, add):
        if u is not None:
            add += n_c * u + n_y * pltpu.roll(u, 127, 1) + n_s * pltpu.roll(u, 1, 1)
        return jnp.where(open_rows, add, 0.0)

    pack_off = iota((128, 128), 1) - 3 * (iota((128, 128), 0) - 3)
    packed = []
    for side, near, far in ((0, n_w, n_x), (1, n_x, n_w)):
        g_side = jnp.concatenate([fine_ghost[48 * a + C * side : 48 * a + C * side + C] for a in range(2)], axis=0)
        lines = response(g_side, near, far, along)
        packed.append(
            sum(
                select_dot(split2(v), one_hot(pack_off == (k if side == 0 else 2 - k)))
                for k, v in enumerate(lines)
            )
        )
    fix_w[...] = packed[0]
    fix_e[...] = packed[1]

    def fix_cols(t, _):
        plane = pl.ds(pl.multiple_of(8 * t, 8), 8)
        w_fix, e_fix = fix_w[plane, :], fix_e[plane, :]
        for f in range(NR):
            res[f, plane, pl.ds(0, 128)] += jnp.where(lane < 3, pltpu.roll(w_fix, (128 - 3 * f) % 128, 1), 0.0)
            res[f, plane, pl.ds(256, 128)] += jnp.where(lane >= 125, pltpu.roll(e_fix, (125 - 3 * f) % 128, 1), 0.0)
        return 0

    lax.fori_loop(0, 6, fix_cols, 0)

    def store_rows(some):
        for r in some:
            cp = pltpu.make_async_copy(res.at[r], nout.at[:, r, :], row_sem.at[r])
            cp.start()
            outs.append(cp)

    store_rows(range(3, NR - 3))
    to_pair(1)
    to_pair(2)
    place(0)

    for e, end in ((0, 0), (1, D - 1)):

        @pl.when(d == end)
        def _(e=e, end=end):
            whole = edge[e]
            for k in range(1, D):
                s = (end + k) % D
                remote(edge.at[e], edge_in.at[s], edge_sem.at[0, e], edge_sem.at[1, s], "dev", end).wait_recv()
            for k in range(1, D):
                whole = whole + edge_in[(end + k) % D]
            off = iota((TC, NC), 1) - 3 * iota((TC, NC), 0)
            spread = jnp.where((off >= 0) & (off < 3), 1.0, 0.0).astype(BF16)
            fine[...] = sum(
                jnp.dot(part, spread, preferred_element_type=F32) for part in split3(whole)
            )

        @pl.when(d != end)
        def _(e=e, end=end):
            remote(edge.at[e], edge_in.at[d], edge_sem.at[0, e], edge_sem.at[1, d], "dev", end).wait_send()


    for e, end in ((0, 0), (1, D - 1)):

        @pl.when(d == end)
        def _(e=e):
            n3 = [jnp.concatenate([v] * 3, axis=1) for v in (n_c, n_x, n_w, n_y, n_s)]
            at = iota((PLANES, NC), 1)

            def over(u, add):
                if u is None:
                    return add
                right = jnp.where(at == NC - 1, 0.0, pltpu.roll(u, NC - 1, 1))
                left = jnp.where(at == 0, 0.0, pltpu.roll(u, 1, 1))
                return n3[0] * u + n3[1] * right + n3[2] * left + add

            near, far = (n3[4], n3[3]) if e == 0 else (n3[3], n3[4])
            for k, v in enumerate(response(fine[...], near, far, over)):
                res[k if e == 0 else NR - 1 - k] += v

    store_rows([0, 1, 2, NR - 3, NR - 2, NR - 1])
    place(1)
    place(2)
    for cp in sends:
        cp.wait_send()
    for cp in outs:
        cp.wait()


def shards(parent, nest, anchor, diffusion, courant):
    any_space = pl.BlockSpec(memory_space=pl.ANY)
    scalars = pl.BlockSpec(memory_space=pltpu.SMEM)
    dma = pltpu.SemaphoreType.DMA
    vmem = pltpu.VMEM
    pout, nout = pl.pallas_call(
        kernel,
        out_shape=(
            pltpu.VMEM((C, TR, TC), F32),
            pltpu.VMEM((PLANES, NR, NC), F32),
        ),
        in_specs=[scalars] * 3 + [pl.BlockSpec(memory_space=pltpu.HBM)] * 2,
        out_specs=(any_space, any_space),
        scratch_shapes=[
            vmem((NR + 6, PLANES, NC), F32),
            vmem((NR, PLANES, NC), F32),
            vmem((C, TR, TC), F32),
            vmem((2, C, 8, TC), F32),
            vmem((2, TR, 128), F32),
            vmem((2, TR, 128), F32),
            vmem((G, TR + PLANES, 128), F32),
            vmem((G, TR + PLANES, 128), F32),
            vmem((LEAD + G * TR + 32, 128), F32),
            vmem((D, 16, 128), F32),
            vmem((D, 16, 128), F32),
            vmem((2, PLANES, 128), F32),
            vmem((D, PLANES, 128), F32),
            vmem((128, 128), F32),
            vmem((PLANES, NC), F32),
            vmem((5, C, 128), F32),
            vmem((128, NC), F32),
            vmem((TR, 128), F32),
            vmem((2, 8, 128), F32),
            vmem((C, 128), F32),
            vmem((2, C, 128), F32),
            vmem((3 * (TR + 16), 128), F32),
            vmem((TR, 128), F32),
            vmem((PLANES, 128), F32),
            vmem((PLANES, 128), F32),
            vmem((3, 2, 8, 8, TC), F32),
            *[vmem((NESTS, 4, 8, TC), F32)] * 3,
            vmem((3, D, 4, 8, TC), F32),
            *[vmem((32, 2, 4, 8, TC), F32)] * 3,
            vmem((8 * TR, TC), F32),
            vmem((C, TR, TC), F32),
            pltpu.SMEM((8,), I32),
            dma((NR,)),
            dma((4,)),
            dma((2, 10)),
            dma((2, G)),
            dma((2, D)),
            dma((2, D)),
            dma((2, 3, G)),
            dma((2, 3, D)),
            dma((2, 3)),
        ],
        compiler_params=pltpu.CompilerParams(
            collective_id=0, has_side_effects=True, vmem_limit_bytes=52 * 1024 * 1024
        ),
    )(anchor.T, diffusion, courant, pltpu.with_memory_space_constraint(parent, pltpu.HBM), pltpu.with_memory_space_constraint(nest.reshape(PLANES, NR, NC), pltpu.HBM))
    return pout, nout.reshape(2, C, NR, NC)


def solution(mesh):
    placed = (P(None, "grp", "dev"), P("grp", None, "dev", None), P(), P(), P())
    return jax.shard_map(
        shards,
        mesh=mesh,
        in_specs=placed,
        out_specs=(P(None, "grp", "dev"), P("grp", None, "dev", None)),
        check_vma=False,
    )
```

```python
import functools

import jax
import jax.numpy as jnp
from jax import lax
from jax.experimental import pallas as pl
from jax.experimental.pallas import tpu as pltpu
from jax.sharding import PartitionSpec as P

F32 = jnp.float32
BF16 = jnp.bfloat16
I32 = jnp.int32
MESH = pl.DeviceIdType.MESH

G = 8
D = 16
C = 24
TR = 64
TC = 128
NR = 24
NC = 384
FP = 128
BAND = 256
NESTS = 16
PLANES = 2 * C
LEAD = 8


def iota(shape, axis):
    return lax.broadcasted_iota(I32, shape, axis)


def remote(src, dst, send, recv, axis, target):
    return pltpu.make_async_remote_copy(
        src_ref=src,
        dst_ref=dst,
        send_sem=send,
        recv_sem=recv,
        device_id={axis: target},
        device_id_type=MESH,
    )


def split3(a):
    hi = a.astype(BF16)
    rest = a - hi.astype(F32)
    mid = rest.astype(BF16)
    return hi, mid, (rest - mid.astype(F32)).astype(BF16)


def response(g, near, far, along):
    push = near * g
    a1 = along(None, push)
    b1 = along(a1, push)
    b2 = along(None, near * a1)
    c1 = along(b1, push + far * b2)
    c2 = along(b2, near * b1)
    c3 = along(None, near * b2)
    return c1, c2, c3


def select_dot(parts, matrix):
    return sum(jnp.dot(part, matrix, preferred_element_type=F32) for part in parts)


def one_hot(mask):
    return jnp.where(mask, 1.0, 0.0).astype(BF16)


def split2(a):
    hi = a.astype(BF16)
    return hi, (a - hi.astype(F32)).astype(BF16)


def kernel(
    anchor,
    diff,
    cour,
    parent,
    nest,
    pout,
    nout,
    work,
    res,
    pv,
    prow_in,
    pcol,
    pcol_in,
    item,
    item_in,
    wecol,
    strip,
    strip_in,
    edge,
    edge_in,
    ghost,
    fine,
    coef,
    triple,
    gcol,
    gcol_in,
    grow,
    grow_in,
    tall,
    col_fix,
    fix_w,
    fix_e,
    avg,
    slabs0,
    slabs1,
    slabs2,
    slab_out,
    canvas0,
    canvas1,
    canvas2,
    window,
    adv,
    tab,
    row_sem,
    local_sem,
    halo_sem,
    item_sem,
    strip_sem,
    edge_sem,
    slab_sem,
    canvas_sem,
    pair_sem,
):
    slabs = (slabs0, slabs1, slabs2)
    canvas = (canvas0, canvas1, canvas2)
    g = lax.axis_index("grp")
    d = lax.axis_index("dev")
    core = lax.rem(g, 2)
    row0 = g * TR
    col0 = d * TC
    lane = iota((1, 128), 1)

    own_parent = pltpu.make_async_copy(parent, pv, local_sem.at[0])
    own_parent.start()
    own_nest = [pltpu.make_async_copy(nest.at[:, r, :], work.at[3 + r], row_sem.at[r]) for r in range(NR)]
    for cp in own_nest:
        cp.start()
    barrier = pltpu.get_barrier_semaphore()
    for k in range(1, G):
        pl.semaphore_signal(barrier, inc=1, device_id={"grp": lax.rem(g + k, G)}, device_id_type=MESH)
    for k in range(1, D):
        pl.semaphore_signal(barrier, inc=1, device_id={"dev": lax.rem(d + k, D)}, device_id_type=MESH)

    for cp in own_nest:
        cp.wait()
    pl.semaphore_wait(barrier, G + D - 2)

    sends = []
    up_g, dn_g = lax.rem(g + 1, G), lax.rem(g + G - 1, G)
    up_d, dn_d = lax.rem(d + 1, D), lax.rem(d + D - 1, D)

    def halo(src, dst, i, axis, target):
        return remote(src, dst, halo_sem.at[0, i], halo_sem.at[1, i], axis, target)

    nest_halo = [
        halo(work.at[pl.ds(NR, 3)], work.at[pl.ds(0, 3)], 4, "dev", up_d),
        halo(work.at[pl.ds(3, 3)], work.at[pl.ds(NR + 3, 3)], 5, "dev", dn_d),
    ]
    parent_halo = [
        halo(parent.at[:, pl.ds(TR - 1, 1), :], prow_in.at[0, :, pl.ds(0, 1), :], 0, "grp", up_g),
        halo(parent.at[:, pl.ds(0, 1), :], prow_in.at[1, :, pl.ds(0, 1), :], 1, "grp", dn_g),
        halo(pcol.at[1], pcol_in.at[0], 2, "dev", up_d),
        halo(pcol.at[0], pcol_in.at[1], 3, "dev", dn_d),
    ]
    line_halo = [
        halo(gcol.at[pl.ds(TR - 8, 8)], gcol_in.at[0], 6, "grp", up_g),
        halo(gcol.at[pl.ds(0, 8)], gcol_in.at[1], 7, "grp", dn_g),
        halo(grow, grow_in.at[0], 8, "dev", up_d),
        halo(grow, grow_in.at[1], 9, "dev", dn_d),
    ]
    for cp in nest_halo + parent_halo[:2]:
        cp.start()

    key = [(anchor[0, n] >> 8) * 8 + (anchor[1, n] >> 8) for n in range(NESTS)]
    band_row = lax.div(g, 4)
    for b in range(8):
        found = jnp.int32(0)
        for n in range(NESTS):
            found = jnp.where(key[n] == band_row * 8 + b, n, found)
        tab[b] = found
    other = jnp.int32(0)
    for n in range(NESTS):
        other = jnp.where(key[n] == (1 - band_row) * 8 + lax.div(d, 2), n, other)
    mine = tab[lax.div(d, 2)]
    odd = lax.rem(d, 2)
    beside = tab[jnp.clip(lax.div(d, 2) - 1 + 2 * odd, 0, 7)]

    r_m, q_m = anchor[0, mine], anchor[1, mine]
    west_m = q_m - 1 - col0
    east_m = q_m + FP - col0
    is_west = (west_m >= 0) & (west_m < TC)
    is_east = (east_m >= 0) & (east_m < TC)
    pick = jnp.where(is_west, west_m, jnp.where(is_east, east_m, 0))
    q_b = anchor[1, beside]
    beside_on = jnp.where(odd == 1, q_b == col0 + TC, q_b + FP == col0)

    south_m = r_m - 1 - row0
    north_m = r_m + FP - row0
    is_south = (south_m >= 0) & (south_m < TR)
    is_north = (north_m >= 0) & (north_m < TR)
    row_pick = jnp.where(is_south, south_m, jnp.where(is_north, north_m, 0))
    r_o, q_o = anchor[0, other], anchor[1, other]
    low = band_row == 0
    other_on = jnp.where(low, r_o == row0 + TR, r_o + FP == row0)

    own_parent.wait()

    def gather(c, carry):
        first, last, picked, row_m, row_o = carry
        x = pv[c]
        here = lane == c
        first = jnp.where(here, pltpu.roll(x, c, 1), first)
        last = jnp.where(here, pltpu.roll(x, c + 1, 1), last)
        picked = jnp.where(here, pltpu.roll(x, (c - pick) & 127, 1), picked)
        sub = iota((C, 128), 0) == c
        row_m = jnp.where(sub, pv[c, pl.ds(row_pick, 1), :], row_m)
        edge_row = jnp.where(low, x[TR - 1 : TR], x[0:1])
        row_o = jnp.where(sub, edge_row, row_o)
        return first, last, picked, row_m, row_o

    zero_col = jnp.zeros((TR, 128), F32)
    zero_row = jnp.zeros((C, 128), F32)
    first, last, picked, row_m, row_o = lax.fori_loop(
        0, C, gather, (zero_col, zero_col, zero_col, zero_row, zero_row)
    )
    pcol[0] = first
    pcol[1] = last
    for cp in parent_halo[2:]:
        cp.start()
    side = jnp.where(odd == 1, last, first)
    place_m = (mine & 1) * 48 + jnp.where(is_west, 0, C)
    place_b = (beside & 1) * 48 + jnp.where(odd == 1, 0, C)
    cols_m = pltpu.roll(picked, place_m, 1)
    cols_b = pltpu.roll(side, place_b, 1)
    span_m = lane + (q_m - col0)
    span_o = lane + (q_o - col0)
    rows_m = jnp.where((span_m >= 0) & (span_m < TC), pltpu.roll(row_m, (col0 - q_m) & 127, 1), 0.0)
    rows_o = jnp.where((span_o >= 0) & (span_o < TC), pltpu.roll(row_o, (col0 - q_o) & 127, 1), 0.0)
    for t in range(G):
        a_m = jnp.where((mine >> 1 == t) & (is_west | is_east), 1, 0)
        a_b = jnp.where((beside >> 1 == t) & beside_on, 1, 0)
        item[t, pl.ds(0, TR), :] = jnp.where(a_m == 1, cols_m, 0.0) + jnp.where(a_b == 1, cols_b, 0.0)
        for a in range(2):
            s_m = jnp.where((mine == 2 * t + a) & (is_south | is_north), 1, 0)
            s_o = jnp.where((other == 2 * t + a) & other_on, 1, 0)
            item[t, pl.ds(TR + C * a, C), :] = jnp.where(s_m == 1, rows_m, 0.0) + jnp.where(
                s_o == 1, rows_o, 0.0
            )

    for k in range(1, G):
        t = lax.rem(g + k, G)
        cp = remote(item.at[t], item_in.at[g], item_sem.at[0, k], item_sem.at[1, k], "grp", t)
        cp.start()
        sends.append(cp)
    item_in[g] = item[g]

    lanes = [jnp.zeros((1, 128), F32)] * 5
    for c in range(C):
        kx, ky = 3.0 * diff[0, c], 3.0 * diff[1, c]
        ax, ay = cour[0, c], cour[1, c]
        here = (lane == c) | (lane == 32 + c)
        for i, v in enumerate((1.0 - 2.0 * kx - 2.0 * ky - ax - ay, kx, kx + ax, ky, ky + ay)):
            coef[i, pl.ds(c, 1), :] = jnp.full((1, 128), v, F32)
            lanes[i] = jnp.where(here, v, lanes[i])

    for cp in nest_halo:
        cp.wait()

    off = iota((NC, TC), 0) - 3 * iota((NC, TC), 1)
    collect = one_hot((off >= 0) & (off < 3))
    first_dev, last_dev = d == 0, d == D - 1
    tiles = range(3)

    def substeps(j, a):
        plane = pl.ds(pl.multiple_of(C * a + 8 * j, 8), 8)
        k_c, k_x, k_w, k_y, k_s = (coef[i, pl.ds(8 * j, 8), :] for i in range(5))
        def keep(w, row):
            if w == 2:
                return [jnp.where(first_dev, 0.0, row[i]) for i in tiles]
            if w == NR + 3:
                return [jnp.where(last_dev, 0.0, row[i]) for i in tiles]
            return row

        def advance(below, row, above):
            right = [0.0] + [pltpu.roll(v, 1, 1) for v in row]
            left = [pltpu.roll(v, 127, 1) for v in row] + [0.0]
            return [
                k_c * row[i]
                + k_x * jnp.where(lane == 127, left[i + 1], left[i])
                + k_w * jnp.where(lane == 0, right[i], right[i + 1])
                + k_y * above[i]
                + k_s * below[i]
                for i in tiles
            ]

        levels = [{}, {}, {}]
        acc = None
        for w in range(NR + 6):
            levels[0][w] = keep(w, [work[w, plane, pl.ds(128 * i, 128)] for i in tiles])
            for n in range(3):
                v = w - n - 1
                if v <= n or v >= NR + 5 - n:
                    continue
                src = levels[n]
                made = advance(src[v - 1], src[v], src[v + 1])
                del src[v - 1]
                if n < 2:
                    levels[n + 1][v] = keep(v, made)
                    continue
                for i in tiles:
                    res[v - 3, plane, pl.ds(128 * i, 128)] = made[i]
                acc = made if (v - 3) % 3 == 0 else [x + y for x, y in zip(acc, made)]
                if (v - 3) % 3 == 2:
                    at = pl.ds(pl.multiple_of(64 * a + 8 * ((v - 3) // 3), 8), 8)
                    for i in tiles:
                        triple[at, pl.ds(128 * i, 128)] = acc[i]

    pair = g + 1 - 2 * core

    def slab_copy(j, k, t, mine_g):
        return remote(
            avg.at[j, :, pl.ds(4 * (lax.rem(t, 2)), 4)],
            slabs[j].at[pl.ds(2 * mine_g, 2)],
            slab_sem.at[0, j, k],
            slab_sem.at[1, j, k],
            "grp",
            t,
        )

    def canvas_copy(j, k, t, mine_d):
        return remote(
            slab_out.at[j, k],
            canvas[j].at[8 + mine_d, core],
            canvas_sem.at[0, j, k],
            canvas_sem.at[1, j, k],
            "dev",
            t,
        )

    def pair_copy(j, half):
        block = canvas[j].at[pl.ds(8, D), half]
        return remote(block, block, pair_sem.at[0, j], pair_sem.at[1, j], "grp", pair)

    def to_groups(j):
        for k in range(1, G):
            cp = slab_copy(j, k, lax.rem(g + k, G), g)
            cp.start()
            sends.append(cp)
        slabs[j][pl.ds(2 * g, 2)] = avg[j, :, pl.ds(4 * core, 4)]

    def to_columns(j):
        for k in range(1, G):
            slab_copy(j, k, g, lax.rem(g + G - k, G)).wait_recv()
        for k in range(1, D):
            t = lax.rem(d + k, D)
            slab_out[j, k] = slabs[j][tab[lax.div(t, 2)]]
            cp = canvas_copy(j, k, t, d)
            cp.start()
            sends.append(cp)
        canvas[j][8 + d, core] = slabs[j][mine]

    def to_pair(j):
        for k in range(1, D):
            canvas_copy(j, k, d, lax.rem(d + D - k, D)).wait_recv()
        cp = pair_copy(j, core)
        cp.start()
        sends.append(cp)

    own_row = jnp.clip(row0 - r_m, -TR, FP) + TR
    shift = (q_m - col0) & 127
    tile_row = iota((TR, 128), 0) + (row0 - r_m)
    tile_col = iota((TR, 128), 1) + (col0 - q_m)
    covered = (tile_row >= 0) & (tile_row < FP) & (tile_col >= 0) & (tile_col < FP)
    rows_of = [c.reshape(256, 8, TC) for c in canvas]
    outs = []

    def place(j):
        pair_copy(j, 1 - core).wait_recv()
        window[...] = rows_of[j][pl.ds(own_row, TR)].reshape(8 * TR, TC)
        for i in range(8):
            c = 8 * j + i
            under = pltpu.roll(window[pl.ds(i, TR, stride=8), :], shift, 1)
            fix = col_fix[...]
            under += jnp.where(lane == at_w, pltpu.roll(fix, (at_w - c) & 127, 1), 0.0)
            under += jnp.where(lane == at_e, pltpu.roll(fix, (at_e - 32 - c) & 127, 1), 0.0)
            under += jnp.where(tile == row_at, row_fix[c : c + 1], 0.0)
            adv[c] = jnp.where(covered, under, adv[c])
        cp = pltpu.make_async_copy(adv.at[pl.ds(8 * j, 8)], pout.at[pl.ds(8 * j, 8)], local_sem.at[1 + j])
        cp.start()
        outs.append(cp)

    def compute(j):
        def one(a, _):
            substeps(j, a)
            return 0

        lax.fori_loop(0, 2, one, 0)
        mean = select_dot(split2(triple[...]), collect) * (1.0 / 9.0)
        avg[j] = mean.reshape(2, 8, 8, TC)
        to_groups(j)

    compute(0)

    for k in range(1, G):
        s = lax.rem(g + G - k, G)
        remote(item.at[s], item_in.at[s], item_sem.at[0, k], item_sem.at[1, k], "grp", s).wait_recv()
    wecol[pl.ds(0, LEAD), :] = jnp.zeros((LEAD, 128), F32)
    wecol[pl.ds(LEAD + G * TR, 32), :] = jnp.zeros((32, 128), F32)
    south = [jnp.zeros((C, 128), F32)] * 2
    north = [jnp.zeros((C, 128), F32)] * 2
    r_own = [anchor[0, 2 * g + a] for a in range(2)]
    for s in range(G):
        wecol[pl.ds(LEAD + s * TR, TR), :] = item_in[s, pl.ds(0, TR), :]
        for a in range(2):
            got = item_in[s, pl.ds(TR + C * a, C), :]
            below = r_own[a] - 1 - s * TR
            above = r_own[a] + FP - s * TR
            south[a] = south[a] + jnp.where((below >= 0) & (below < TR), got, 0.0)
            north[a] = north[a] + jnp.where((above >= 0) & (above < TR), got, 0.0)
    for a in range(2):
        edge[0, pl.ds(C * a, C), :] = south[a]
        edge[1, pl.ds(C * a, C), :] = north[a]

    def strip_of(t):
        parts = [wecol[pl.ds(LEAD - 1 + r_own[a] + 8 * t, 16), :] for a in range(2)]
        return jnp.where(lane < 48, parts[0], parts[1])

    for k in range(1, D):
        t = lax.rem(d + k, D)
        strip[k] = strip_of(t)
        cp = remote(strip.at[k], strip_in.at[k], strip_sem.at[0, k], strip_sem.at[1, k], "dev", t)
        cp.start()
        sends.append(cp)
    strip_in[0] = strip_of(d)

    for e, end in ((0, 0), (1, D - 1)):

        @pl.when(d != end)
        def _(e=e, end=end):
            remote(edge.at[e], edge_in.at[d], edge_sem.at[0, e], edge_sem.at[1, d], "dev", end).start()


    compute(1)

    for cp in parent_halo:
        cp.wait()
    at_w, at_e = q_m - col0, q_m + FP - 1 - col0
    at_s, at_n = r_m - row0, r_m + FP - 1 - row0
    from_w = jnp.where(d == 0, 0.0, pcol_in[0])
    from_e = jnp.where(d == D - 1, 0.0, pcol_in[1])
    line_w = jnp.where(at_w == 0, from_w, picked)
    line_e = jnp.where(at_e == TC - 1, from_e, picked)
    gcol[...] = jnp.where(lane < 32, line_w, pltpu.roll(line_e, 32, 1))
    has_s = (at_s >= 0) & (at_s < TR)
    from_s = jnp.where(g == 0, 0.0, prow_in[0, :, 0, :])
    from_n = jnp.where(g == G - 1, 0.0, prow_in[1, :, 0, :])
    grow[...] = jnp.where(at_s == 0, from_s, jnp.where(at_n == TR - 1, from_n, row_m))
    for cp in line_halo:
        cp.start()

    compute(2)

    to_columns(0)

    to_columns(1)

    to_columns(2)

    tile = iota((TR, 128), 0)

    def parent_step(c, _):
        mid = pv[c]
        kx, ky = diff[0, c], diff[1, c]
        ax, ay = cour[0, c], cour[1, c]
        gw = jnp.where(d == 0, 0.0, pltpu.roll(pcol_in[0], (128 - c) & 127, 1))
        ge = jnp.where(d == D - 1, 0.0, pltpu.roll(pcol_in[1], 127 - c, 1))
        gs = jnp.where(g == 0, 0.0, prow_in[0, c, 0:1, :])
        gn = jnp.where(g == G - 1, 0.0, prow_in[1, c, 0:1, :])
        west = jnp.where(lane == 0, gw, pltpu.roll(mid, 1, 1))
        east = jnp.where(lane == 127, ge, pltpu.roll(mid, 127, 1))
        below = jnp.where(tile == 0, gs, pltpu.roll(mid, 1, 0))
        above = jnp.where(tile == TR - 1, gn, pltpu.roll(mid, TR - 1, 0))
        adv[c] = (
            mid * (1.0 - 2.0 * kx - 2.0 * ky - ax - ay)
            + kx * east
            + (kx + ax) * west
            + ky * above
            + (ky + ay) * below
        )
        return 0

    lax.fori_loop(0, C, parent_step, 0)


    for cp in line_halo:
        cp.wait()
    column = jnp.concatenate([gcol_in[0], gcol[...], gcol_in[1]], axis=0)
    for k in range(3):
        tall[pl.ds(k, TR + 16, stride=3), :] = column
    tall_row = iota((3 * (TR + 16), 128), 0) + 3 * (row0 - r_m - 8)
    inside = (tall_row >= 0) & (tall_row < NC)
    l_c, l_x, l_w, l_y, l_s = lanes
    size = 3 * (TR + 16)

    def down(u, add):
        if u is not None:
            add += l_c * u + l_y * pltpu.roll(u, size - 1, 0) + l_s * pltpu.roll(u, 1, 0)
        return jnp.where(inside, add, 0.0)

    w_lane = lane < 32
    tall[...] = sum(response(tall[...], jnp.where(w_lane, l_w, l_x), jnp.where(w_lane, l_x, l_w), down))
    col_fix[...] = sum(tall[pl.ds(24 + k, TR, stride=3), :] for k in range(3)) * (1.0 / 9.0)

    wide = 512
    wide_off = iota((TC, wide), 1) - 64 - 3 * iota((TC, wide), 0)
    to_wide = [one_hot((wide_off + o >= 0) & (wide_off + o < 3)) for o in (NC, 0, -NC)]
    row = sum(
        select_dot(split3(v), m) for v, m in zip((grow_in[0], grow[...], grow_in[1]), to_wide)
    )
    wide_col = iota((C, wide), 1) - 64 + 3 * (col0 - q_m)
    within = (wide_col >= 0) & (wide_col < NC)
    c_c, c_x, c_w, c_y, c_s = (jnp.concatenate([coef[i]] * 4, axis=1) for i in range(5))

    def across(u, add):
        if u is not None:
            add += c_c * u + c_x * pltpu.roll(u, wide - 1, 1) + c_w * pltpu.roll(u, 1, 1)
        return jnp.where(within, add, 0.0)

    strip_sum = sum(response(row, jnp.where(has_s, c_s, c_y), jnp.where(has_s, c_y, c_s), across))
    back = iota((wide, TC), 0) - 64 - 3 * iota((wide, TC), 1)
    row_fix = select_dot(split2(strip_sum), one_hot((back >= 0) & (back < 3))) * (1.0 / 9.0)
    row_at = jnp.where(has_s, at_s, at_n)

    to_pair(0)

    for k in range(1, D):
        remote(strip.at[k], strip_in.at[k], strip_sem.at[0, k], strip_sem.at[1, k], "dev", d).wait_recv()
    total = strip_in[0]
    for k in range(1, D):
        total = total + strip_in[k]
    ghost[...] = jnp.transpose(jnp.concatenate([total, jnp.zeros((112, 128), F32)], axis=0))

    spread_off = iota((128, 128), 1) - 3 * iota((128, 128), 0)
    fine_ghost = select_dot(split3(ghost[...]), one_hot((spread_off >= 0) & (spread_off < 3)))
    open_rows = ((lane >= 3) | (d != 0)) & ((lane < NR + 3) | (d != D - 1)) & (lane < NR + 6)
    n_c, n_x, n_w, n_y, n_s = (jnp.concatenate([coef[i]] * 2, axis=0) for i in range(5))

    def along(u, add):
        if u is not None:
            add += n_c * u + n_y * pltpu.roll(u, 127, 1) + n_s * pltpu.roll(u, 1, 1)
        return jnp.where(open_rows, add, 0.0)

    pack_off = iota((128, 128), 1) - 3 * (iota((128, 128), 0) - 3)
    packed = []
    for side, near, far in ((0, n_w, n_x), (1, n_x, n_w)):
        g_side = jnp.concatenate([fine_ghost[48 * a + C * side : 48 * a + C * side + C] for a in range(2)], axis=0)
        lines = response(g_side, near, far, along)
        packed.append(
            sum(
                select_dot(split2(v), one_hot(pack_off == (k if side == 0 else 2 - k)))
                for k, v in enumerate(lines)
            )
        )
    fix_w[...] = packed[0]
    fix_e[...] = packed[1]

    def fix_cols(t, _):
        plane = pl.ds(pl.multiple_of(8 * t, 8), 8)
        w_fix, e_fix = fix_w[plane, :], fix_e[plane, :]
        for f in range(NR):
            res[f, plane, pl.ds(0, 128)] += jnp.where(lane < 3, pltpu.roll(w_fix, (128 - 3 * f) % 128, 1), 0.0)
            res[f, plane, pl.ds(256, 128)] += jnp.where(lane >= 125, pltpu.roll(e_fix, (125 - 3 * f) % 128, 1), 0.0)
        return 0

    lax.fori_loop(0, 6, fix_cols, 0)

    def store_rows(some):
        for r in some:
            cp = pltpu.make_async_copy(res.at[r], nout.at[:, r, :], row_sem.at[r])
            cp.start()
            outs.append(cp)

    store_rows(range(3, NR - 3))
    to_pair(1)
    to_pair(2)
    place(0)

    for e, end in ((0, 0), (1, D - 1)):

        @pl.when(d == end)
        def _(e=e, end=end):
            whole = edge[e]
            for k in range(1, D):
                s = (end + k) % D
                remote(edge.at[e], edge_in.at[s], edge_sem.at[0, e], edge_sem.at[1, s], "dev", end).wait_recv()
            for k in range(1, D):
                whole = whole + edge_in[(end + k) % D]
            off = iota((TC, NC), 1) - 3 * iota((TC, NC), 0)
            spread = jnp.where((off >= 0) & (off < 3), 1.0, 0.0).astype(BF16)
            fine[...] = sum(
                jnp.dot(part, spread, preferred_element_type=F32) for part in split3(whole)
            )

        @pl.when(d != end)
        def _(e=e, end=end):
            remote(edge.at[e], edge_in.at[d], edge_sem.at[0, e], edge_sem.at[1, d], "dev", end).wait_send()


    for e, end in ((0, 0), (1, D - 1)):

        @pl.when(d == end)
        def _(e=e):
            n3 = [jnp.concatenate([v] * 3, axis=1) for v in (n_c, n_x, n_w, n_y, n_s)]
            at = iota((PLANES, NC), 1)

            def over(u, add):
                if u is None:
                    return add
                right = jnp.where(at == NC - 1, 0.0, pltpu.roll(u, NC - 1, 1))
                left = jnp.where(at == 0, 0.0, pltpu.roll(u, 1, 1))
                return n3[0] * u + n3[1] * right + n3[2] * left + add

            near, far = (n3[4], n3[3]) if e == 0 else (n3[3], n3[4])
            for k, v in enumerate(response(fine[...], near, far, over)):
                res[k if e == 0 else NR - 1 - k] += v

    store_rows([0, 1, 2, NR - 3, NR - 2, NR - 1])
    place(1)
    place(2)
    for cp in sends:
        cp.wait_send()
    for cp in outs:
        cp.wait()


def shards(parent, nest, anchor, diffusion, courant):
    any_space = pl.BlockSpec(memory_space=pl.ANY)
    scalars = pl.BlockSpec(memory_space=pltpu.SMEM)
    dma = pltpu.SemaphoreType.DMA
    vmem = pltpu.VMEM
    pout, nout = pl.pallas_call(
        kernel,
        out_shape=(
            pltpu.VMEM((C, TR, TC), F32),
            pltpu.VMEM((PLANES, NR, NC), F32),
        ),
        in_specs=[scalars] * 3 + [pl.BlockSpec(memory_space=pltpu.HBM)] * 2,
        out_specs=(any_space, any_space),
        scratch_shapes=[
            vmem((NR + 6, PLANES, NC), F32),
            vmem((NR, PLANES, NC), F32),
            vmem((C, TR, TC), F32),
            vmem((2, C, 8, TC), F32),
            vmem((2, TR, 128), F32),
            vmem((2, TR, 128), F32),
            vmem((G, TR + PLANES, 128), F32),
            vmem((G, TR + PLANES, 128), F32),
            vmem((LEAD + G * TR + 32, 128), F32),
            vmem((D, 16, 128), F32),
            vmem((D, 16, 128), F32),
            vmem((2, PLANES, 128), F32),
            vmem((D, PLANES, 128), F32),
            vmem((128, 128), F32),
            vmem((PLANES, NC), F32),
            vmem((5, C, 128), F32),
            vmem((128, NC), F32),
            vmem((TR, 128), F32),
            vmem((2, 8, 128), F32),
            vmem((C, 128), F32),
            vmem((2, C, 128), F32),
            vmem((3 * (TR + 16), 128), F32),
            vmem((TR, 128), F32),
            vmem((PLANES, 128), F32),
            vmem((PLANES, 128), F32),
            vmem((3, 2, 8, 8, TC), F32),
            *[vmem((NESTS, 4, 8, TC), F32)] * 3,
            vmem((3, D, 4, 8, TC), F32),
            *[vmem((32, 2, 4, 8, TC), F32)] * 3,
            vmem((8 * TR, TC), F32),
            vmem((C, TR, TC), F32),
            pltpu.SMEM((8,), I32),
            dma((NR,)),
            dma((4,)),
            dma((2, 10)),
            dma((2, G)),
            dma((2, D)),
            dma((2, D)),
            dma((2, 3, G)),
            dma((2, 3, D)),
            dma((2, 3)),
        ],
        compiler_params=pltpu.CompilerParams(
            collective_id=0, has_side_effects=True, vmem_limit_bytes=52 * 1024 * 1024
        ),
    )(anchor.T, diffusion, courant, pltpu.with_memory_space_constraint(parent, pltpu.HBM), pltpu.with_memory_space_constraint(nest.reshape(PLANES, NR, NC), pltpu.HBM))
    return pout, nout.reshape(2, C, NR, NC)


def solution(mesh):
    placed = (P(None, "grp", "dev"), P("grp", None, "dev", None), P(), P(), P())
    return jax.shard_map(
        shards,
        mesh=mesh,
        in_specs=placed,
        out_specs=(P(None, "grp", "dev"), P("grp", None, "dev", None)),
        check_vma=False,
    )
```

```python
import functools

import jax
import jax.numpy as jnp
from jax import lax
from jax.experimental import pallas as pl
from jax.experimental.pallas import tpu as pltpu
from jax.sharding import PartitionSpec as P

F32 = jnp.float32
BF16 = jnp.bfloat16
I32 = jnp.int32
MESH = pl.DeviceIdType.MESH

G = 8
D = 16
C = 24
TR = 64
TC = 128
NR = 24
NC = 384
FP = 128
BAND = 256
NESTS = 16
PLANES = 2 * C
LEAD = 8


def iota(shape, axis):
    return lax.broadcasted_iota(I32, shape, axis)


def remote(src, dst, send, recv, axis, target):
    return pltpu.make_async_remote_copy(
        src_ref=src,
        dst_ref=dst,
        send_sem=send,
        recv_sem=recv,
        device_id={axis: target},
        device_id_type=MESH,
    )


def split3(a):
    hi = a.astype(BF16)
    rest = a - hi.astype(F32)
    mid = rest.astype(BF16)
    return hi, mid, (rest - mid.astype(F32)).astype(BF16)


def response(g, near, far, along):
    push = near * g
    a1 = along(None, push)
    b1 = along(a1, push)
    b2 = along(None, near * a1)
    c1 = along(b1, push + far * b2)
    c2 = along(b2, near * b1)
    c3 = along(None, near * b2)
    return c1, c2, c3


def select_dot(parts, matrix):
    return sum(jnp.dot(part, matrix, preferred_element_type=F32) for part in parts)


def one_hot(mask):
    return jnp.where(mask, 1.0, 0.0).astype(BF16)


def split2(a):
    hi = a.astype(BF16)
    return hi, (a - hi.astype(F32)).astype(BF16)


def kernel(
    anchor,
    diff,
    cour,
    parent,
    nest,
    pout,
    nout,
    work,
    res,
    pv,
    prow_in,
    pcol,
    pcol_in,
    item,
    item_in,
    wecol,
    strip,
    strip_in,
    edge,
    edge_in,
    ghost,
    fine,
    coef,
    triple,
    gcol,
    gcol_in,
    grow,
    grow_in,
    tall,
    col_fix,
    fix_w,
    fix_e,
    avg,
    slabs0,
    slabs1,
    slabs2,
    slab_out,
    canvas0,
    canvas1,
    canvas2,
    window,
    adv,
    tab,
    row_sem,
    local_sem,
    halo_sem,
    item_sem,
    strip_sem,
    edge_sem,
    slab_sem,
    canvas_sem,
    pair_sem,
):
    slabs = (slabs0, slabs1, slabs2)
    canvas = (canvas0, canvas1, canvas2)
    g = lax.axis_index("grp")
    d = lax.axis_index("dev")
    core = lax.rem(g, 2)
    row0 = g * TR
    col0 = d * TC
    lane = iota((1, 128), 1)

    own_parent = pltpu.make_async_copy(parent, pv, local_sem.at[0])
    own_parent.start()
    own_nest = [pltpu.make_async_copy(nest.at[:, r, :], work.at[3 + r], row_sem.at[r]) for r in range(NR)]
    for cp in own_nest:
        cp.start()
    barrier = pltpu.get_barrier_semaphore()
    for k in range(1, G):
        pl.semaphore_signal(barrier, inc=1, device_id={"grp": lax.rem(g + k, G)}, device_id_type=MESH)
    for k in range(1, D):
        pl.semaphore_signal(barrier, inc=1, device_id={"dev": lax.rem(d + k, D)}, device_id_type=MESH)

    for cp in own_nest:
        cp.wait()
    pl.semaphore_wait(barrier, G + D - 2)

    sends = []
    up_g, dn_g = lax.rem(g + 1, G), lax.rem(g + G - 1, G)
    up_d, dn_d = lax.rem(d + 1, D), lax.rem(d + D - 1, D)

    def halo(src, dst, i, axis, target):
        return remote(src, dst, halo_sem.at[0, i], halo_sem.at[1, i], axis, target)

    nest_halo = [
        halo(work.at[pl.ds(NR, 3)], work.at[pl.ds(0, 3)], 4, "dev", up_d),
        halo(work.at[pl.ds(3, 3)], work.at[pl.ds(NR + 3, 3)], 5, "dev", dn_d),
    ]
    parent_halo = [
        halo(parent.at[:, pl.ds(TR - 1, 1), :], prow_in.at[0, :, pl.ds(0, 1), :], 0, "grp", up_g),
        halo(parent.at[:, pl.ds(0, 1), :], prow_in.at[1, :, pl.ds(0, 1), :], 1, "grp", dn_g),
        halo(pcol.at[1], pcol_in.at[0], 2, "dev", up_d),
        halo(pcol.at[0], pcol_in.at[1], 3, "dev", dn_d),
    ]
    line_halo = [
        halo(gcol.at[pl.ds(TR - 8, 8)], gcol_in.at[0], 6, "grp", up_g),
        halo(gcol.at[pl.ds(0, 8)], gcol_in.at[1], 7, "grp", dn_g),
        halo(grow, grow_in.at[0], 8, "dev", up_d),
        halo(grow, grow_in.at[1], 9, "dev", dn_d),
    ]
    for cp in nest_halo + parent_halo[:2]:
        cp.start()

    key = [(anchor[0, n] >> 8) * 8 + (anchor[1, n] >> 8) for n in range(NESTS)]
    band_row = lax.div(g, 4)
    for b in range(8):
        found = jnp.int32(0)
        for n in range(NESTS):
            found = jnp.where(key[n] == band_row * 8 + b, n, found)
        tab[b] = found
    other = jnp.int32(0)
    for n in range(NESTS):
        other = jnp.where(key[n] == (1 - band_row) * 8 + lax.div(d, 2), n, other)
    mine = tab[lax.div(d, 2)]
    odd = lax.rem(d, 2)
    beside = tab[jnp.clip(lax.div(d, 2) - 1 + 2 * odd, 0, 7)]

    r_m, q_m = anchor[0, mine], anchor[1, mine]
    west_m = q_m - 1 - col0
    east_m = q_m + FP - col0
    is_west = (west_m >= 0) & (west_m < TC)
    is_east = (east_m >= 0) & (east_m < TC)
    pick = jnp.where(is_west, west_m, jnp.where(is_east, east_m, 0))
    q_b = anchor[1, beside]
    beside_on = jnp.where(odd == 1, q_b == col0 + TC, q_b + FP == col0)

    south_m = r_m - 1 - row0
    north_m = r_m + FP - row0
    is_south = (south_m >= 0) & (south_m < TR)
    is_north = (north_m >= 0) & (north_m < TR)
    row_pick = jnp.where(is_south, south_m, jnp.where(is_north, north_m, 0))
    r_o, q_o = anchor[0, other], anchor[1, other]
    low = band_row == 0
    other_on = jnp.where(low, r_o == row0 + TR, r_o + FP == row0)

    own_parent.wait()

    def gather(c, carry):
        first, last, picked, row_m, row_o = carry
        x = pv[c]
        here = lane == c
        first = jnp.where(here, pltpu.roll(x, c, 1), first)
        last = jnp.where(here, pltpu.roll(x, c + 1, 1), last)
        picked = jnp.where(here, pltpu.roll(x, (c - pick) & 127, 1), picked)
        sub = iota((C, 128), 0) == c
        row_m = jnp.where(sub, pv[c, pl.ds(row_pick, 1), :], row_m)
        edge_row = jnp.where(low, x[TR - 1 : TR], x[0:1])
        row_o = jnp.where(sub, edge_row, row_o)
        return first, last, picked, row_m, row_o

    zero_col = jnp.zeros((TR, 128), F32)
    zero_row = jnp.zeros((C, 128), F32)
    first, last, picked, row_m, row_o = lax.fori_loop(
        0, C, gather, (zero_col, zero_col, zero_col, zero_row, zero_row)
    )
    pcol[0] = first
    pcol[1] = last
    for cp in parent_halo[2:]:
        cp.start()
    side = jnp.where(odd == 1, last, first)
    place_m = (mine & 1) * 48 + jnp.where(is_west, 0, C)
    place_b = (beside & 1) * 48 + jnp.where(odd == 1, 0, C)
    cols_m = pltpu.roll(picked, place_m, 1)
    cols_b = pltpu.roll(side, place_b, 1)
    span_m = lane + (q_m - col0)
    span_o = lane + (q_o - col0)
    rows_m = jnp.where((span_m >= 0) & (span_m < TC), pltpu.roll(row_m, (col0 - q_m) & 127, 1), 0.0)
    rows_o = jnp.where((span_o >= 0) & (span_o < TC), pltpu.roll(row_o, (col0 - q_o) & 127, 1), 0.0)
    for t in range(G):
        a_m = jnp.where((mine >> 1 == t) & (is_west | is_east), 1, 0)
        a_b = jnp.where((beside >> 1 == t) & beside_on, 1, 0)
        item[t, pl.ds(0, TR), :] = jnp.where(a_m == 1, cols_m, 0.0) + jnp.where(a_b == 1, cols_b, 0.0)
        for a in range(2):
            s_m = jnp.where((mine == 2 * t + a) & (is_south | is_north), 1, 0)
            s_o = jnp.where((other == 2 * t + a) & other_on, 1, 0)
            item[t, pl.ds(TR + C * a, C), :] = jnp.where(s_m == 1, rows_m, 0.0) + jnp.where(
                s_o == 1, rows_o, 0.0
            )

    for k in range(1, G):
        t = lax.rem(g + k, G)
        cp = remote(item.at[t], item_in.at[g], item_sem.at[0, k], item_sem.at[1, k], "grp", t)
        cp.start()
        sends.append(cp)
    item_in[g] = item[g]

    lanes = [jnp.zeros((1, 128), F32)] * 5
    for c in range(C):
        kx, ky = 3.0 * diff[0, c], 3.0 * diff[1, c]
        ax, ay = cour[0, c], cour[1, c]
        here = (lane == c) | (lane == 32 + c)
        for i, v in enumerate((1.0 - 2.0 * kx - 2.0 * ky - ax - ay, kx, kx + ax, ky, ky + ay)):
            coef[i, pl.ds(c, 1), :] = jnp.full((1, 128), v, F32)
            lanes[i] = jnp.where(here, v, lanes[i])

    for cp in nest_halo:
        cp.wait()

    off = iota((NC, TC), 0) - 3 * iota((NC, TC), 1)
    collect = one_hot((off >= 0) & (off < 3))
    first_dev, last_dev = d == 0, d == D - 1
    tiles = range(3)

    def substeps(j, a):
        plane = pl.ds(pl.multiple_of(C * a + 8 * j, 8), 8)
        k_c, k_x, k_w, k_y, k_s = (coef[i, pl.ds(8 * j, 8), :] for i in range(5))
        def keep(w, row):
            if w == 2:
                return [jnp.where(first_dev, 0.0, row[i]) for i in tiles]
            if w == NR + 3:
                return [jnp.where(last_dev, 0.0, row[i]) for i in tiles]
            return row

        def advance(below, row, above):
            right = [0.0] + [pltpu.roll(v, 1, 1) for v in row]
            left = [pltpu.roll(v, 127, 1) for v in row] + [0.0]
            return [
                k_c * row[i]
                + k_x * jnp.where(lane == 127, left[i + 1], left[i])
                + k_w * jnp.where(lane == 0, right[i], right[i + 1])
                + k_y * above[i]
                + k_s * below[i]
                for i in tiles
            ]

        levels = [{}, {}, {}]
        acc = None
        for w in range(NR + 6):
            levels[0][w] = keep(w, [work[w, plane, pl.ds(128 * i, 128)] for i in tiles])
            for n in range(3):
                v = w - n - 1
                if v <= n or v >= NR + 5 - n:
                    continue
                src = levels[n]
                made = advance(src[v - 1], src[v], src[v + 1])
                del src[v - 1]
                if n < 2:
                    levels[n + 1][v] = keep(v, made)
                    continue
                for i in tiles:
                    res[v - 3, plane, pl.ds(128 * i, 128)] = made[i]
                acc = made if (v - 3) % 3 == 0 else [x + y for x, y in zip(acc, made)]
                if (v - 3) % 3 == 2:
                    at = pl.ds(pl.multiple_of(64 * a + 8 * ((v - 3) // 3), 8), 8)
                    for i in tiles:
                        triple[at, pl.ds(128 * i, 128)] = acc[i]

    pair = g + 1 - 2 * core

    def slab_copy(j, k, t, mine_g):
        return remote(
            avg.at[j, :, pl.ds(4 * (lax.rem(t, 2)), 4)],
            slabs[j].at[pl.ds(2 * mine_g, 2)],
            slab_sem.at[0, j, k],
            slab_sem.at[1, j, k],
            "grp",
            t,
        )

    def canvas_copy(j, k, t, mine_d):
        return remote(
            slab_out.at[j, k],
            canvas[j].at[8 + mine_d, core],
            canvas_sem.at[0, j, k],
            canvas_sem.at[1, j, k],
            "dev",
            t,
        )

    def pair_copy(j, half):
        block = canvas[j].at[pl.ds(8, D), half]
        return remote(block, block, pair_sem.at[0, j], pair_sem.at[1, j], "grp", pair)

    def to_groups(j):
        for k in (4, 3, 5, 2, 6, 7, 1):
            cp = slab_copy(j, k, lax.rem(g + k, G), g)
            cp.start()
            sends.append(cp)
        slabs[j][pl.ds(2 * g, 2)] = avg[j, :, pl.ds(4 * core, 4)]

    def to_columns(j):
        for k in range(1, G):
            slab_copy(j, k, g, lax.rem(g + G - k, G)).wait_recv()
        for k in (10, 9, 11, 6, 14, 8, 2, 5, 7, 13, 15, 3, 12, 4, 1):
            t = lax.rem(d + k, D)
            slab_out[j, k] = slabs[j][tab[lax.div(t, 2)]]
            cp = canvas_copy(j, k, t, d)
            cp.start()
            sends.append(cp)
        canvas[j][8 + d, core] = slabs[j][mine]

    def to_pair(j):
        for k in range(1, D):
            canvas_copy(j, k, d, lax.rem(d + D - k, D)).wait_recv()
        cp = pair_copy(j, core)
        cp.start()
        sends.append(cp)

    own_row = jnp.clip(row0 - r_m, -TR, FP) + TR
    shift = (q_m - col0) & 127
    tile_row = iota((TR, 128), 0) + (row0 - r_m)
    tile_col = iota((TR, 128), 1) + (col0 - q_m)
    covered = (tile_row >= 0) & (tile_row < FP) & (tile_col >= 0) & (tile_col < FP)
    rows_of = [c.reshape(256, 8, TC) for c in canvas]
    outs = []

    def place(j):
        pair_copy(j, 1 - core).wait_recv()
        window[...] = rows_of[j][pl.ds(own_row, TR)].reshape(8 * TR, TC)
        for i in range(8):
            c = 8 * j + i
            under = pltpu.roll(window[pl.ds(i, TR, stride=8), :], shift, 1)
            fix = col_fix[...]
            under += jnp.where(lane == at_w, pltpu.roll(fix, (at_w - c) & 127, 1), 0.0)
            under += jnp.where(lane == at_e, pltpu.roll(fix, (at_e - 32 - c) & 127, 1), 0.0)
            under += jnp.where(tile == row_at, row_fix[c : c + 1], 0.0)
            adv[c] = jnp.where(covered, under, adv[c])
        cp = pltpu.make_async_copy(adv.at[pl.ds(8 * j, 8)], pout.at[pl.ds(8 * j, 8)], local_sem.at[1 + j])
        cp.start()
        outs.append(cp)

    def compute(j):
        def one(a, _):
            substeps(j, a)
            return 0

        lax.fori_loop(0, 2, one, 0)
        mean = select_dot(split2(triple[...]), collect) * (1.0 / 9.0)
        avg[j] = mean.reshape(2, 8, 8, TC)
        to_groups(j)

    compute(0)

    for k in range(1, G):
        s = lax.rem(g + G - k, G)
        remote(item.at[s], item_in.at[s], item_sem.at[0, k], item_sem.at[1, k], "grp", s).wait_recv()
    wecol[pl.ds(0, LEAD), :] = jnp.zeros((LEAD, 128), F32)
    wecol[pl.ds(LEAD + G * TR, 32), :] = jnp.zeros((32, 128), F32)
    south = [jnp.zeros((C, 128), F32)] * 2
    north = [jnp.zeros((C, 128), F32)] * 2
    r_own = [anchor[0, 2 * g + a] for a in range(2)]
    for s in range(G):
        wecol[pl.ds(LEAD + s * TR, TR), :] = item_in[s, pl.ds(0, TR), :]
        for a in range(2):
            got = item_in[s, pl.ds(TR + C * a, C), :]
            below = r_own[a] - 1 - s * TR
            above = r_own[a] + FP - s * TR
            south[a] = south[a] + jnp.where((below >= 0) & (below < TR), got, 0.0)
            north[a] = north[a] + jnp.where((above >= 0) & (above < TR), got, 0.0)
    for a in range(2):
        edge[0, pl.ds(C * a, C), :] = south[a]
        edge[1, pl.ds(C * a, C), :] = north[a]

    def strip_of(t):
        parts = [wecol[pl.ds(LEAD - 1 + r_own[a] + 8 * t, 16), :] for a in range(2)]
        return jnp.where(lane < 48, parts[0], parts[1])

    for k in range(1, D):
        t = lax.rem(d + k, D)
        strip[k] = strip_of(t)
        cp = remote(strip.at[k], strip_in.at[k], strip_sem.at[0, k], strip_sem.at[1, k], "dev", t)
        cp.start()
        sends.append(cp)
    strip_in[0] = strip_of(d)

    for e, end in ((0, 0), (1, D - 1)):

        @pl.when(d != end)
        def _(e=e, end=end):
            remote(edge.at[e], edge_in.at[d], edge_sem.at[0, e], edge_sem.at[1, d], "dev", end).start()


    compute(1)

    for cp in parent_halo:
        cp.wait()
    at_w, at_e = q_m - col0, q_m + FP - 1 - col0
    at_s, at_n = r_m - row0, r_m + FP - 1 - row0
    from_w = jnp.where(d == 0, 0.0, pcol_in[0])
    from_e = jnp.where(d == D - 1, 0.0, pcol_in[1])
    line_w = jnp.where(at_w == 0, from_w, picked)
    line_e = jnp.where(at_e == TC - 1, from_e, picked)
    gcol[...] = jnp.where(lane < 32, line_w, pltpu.roll(line_e, 32, 1))
    has_s = (at_s >= 0) & (at_s < TR)
    from_s = jnp.where(g == 0, 0.0, prow_in[0, :, 0, :])
    from_n = jnp.where(g == G - 1, 0.0, prow_in[1, :, 0, :])
    grow[...] = jnp.where(at_s == 0, from_s, jnp.where(at_n == TR - 1, from_n, row_m))
    for cp in line_halo:
        cp.start()

    compute(2)

    to_columns(0)

    to_columns(1)

    to_columns(2)

    tile = iota((TR, 128), 0)

    def parent_step(c, _):
        mid = pv[c]
        kx, ky = diff[0, c], diff[1, c]
        ax, ay = cour[0, c], cour[1, c]
        gw = jnp.where(d == 0, 0.0, pltpu.roll(pcol_in[0], (128 - c) & 127, 1))
        ge = jnp.where(d == D - 1, 0.0, pltpu.roll(pcol_in[1], 127 - c, 1))
        gs = jnp.where(g == 0, 0.0, prow_in[0, c, 0:1, :])
        gn = jnp.where(g == G - 1, 0.0, prow_in[1, c, 0:1, :])
        west = jnp.where(lane == 0, gw, pltpu.roll(mid, 1, 1))
        east = jnp.where(lane == 127, ge, pltpu.roll(mid, 127, 1))
        below = jnp.where(tile == 0, gs, pltpu.roll(mid, 1, 0))
        above = jnp.where(tile == TR - 1, gn, pltpu.roll(mid, TR - 1, 0))
        adv[c] = (
            mid * (1.0 - 2.0 * kx - 2.0 * ky - ax - ay)
            + kx * east
            + (kx + ax) * west
            + ky * above
            + (ky + ay) * below
        )
        return 0

    lax.fori_loop(0, C, parent_step, 0)


    for cp in line_halo:
        cp.wait()
    column = jnp.concatenate([gcol_in[0], gcol[...], gcol_in[1]], axis=0)
    for k in range(3):
        tall[pl.ds(k, TR + 16, stride=3), :] = column
    tall_row = iota((3 * (TR + 16), 128), 0) + 3 * (row0 - r_m - 8)
    inside = (tall_row >= 0) & (tall_row < NC)
    l_c, l_x, l_w, l_y, l_s = lanes
    size = 3 * (TR + 16)

    def down(u, add):
        if u is not None:
            add += l_c * u + l_y * pltpu.roll(u, size - 1, 0) + l_s * pltpu.roll(u, 1, 0)
        return jnp.where(inside, add, 0.0)

    w_lane = lane < 32
    tall[...] = sum(response(tall[...], jnp.where(w_lane, l_w, l_x), jnp.where(w_lane, l_x, l_w), down))
    col_fix[...] = sum(tall[pl.ds(24 + k, TR, stride=3), :] for k in range(3)) * (1.0 / 9.0)

    wide = 512
    wide_off = iota((TC, wide), 1) - 64 - 3 * iota((TC, wide), 0)
    to_wide = [one_hot((wide_off + o >= 0) & (wide_off + o < 3)) for o in (NC, 0, -NC)]
    row = sum(
        select_dot(split3(v), m) for v, m in zip((grow_in[0], grow[...], grow_in[1]), to_wide)
    )
    wide_col = iota((C, wide), 1) - 64 + 3 * (col0 - q_m)
    within = (wide_col >= 0) & (wide_col < NC)
    c_c, c_x, c_w, c_y, c_s = (jnp.concatenate([coef[i]] * 4, axis=1) for i in range(5))

    def across(u, add):
        if u is not None:
            add += c_c * u + c_x * pltpu.roll(u, wide - 1, 1) + c_w * pltpu.roll(u, 1, 1)
        return jnp.where(within, add, 0.0)

    strip_sum = sum(response(row, jnp.where(has_s, c_s, c_y), jnp.where(has_s, c_y, c_s), across))
    back = iota((wide, TC), 0) - 64 - 3 * iota((wide, TC), 1)
    row_fix = select_dot(split2(strip_sum), one_hot((back >= 0) & (back < 3))) * (1.0 / 9.0)
    row_at = jnp.where(has_s, at_s, at_n)

    to_pair(0)

    for k in range(1, D):
        remote(strip.at[k], strip_in.at[k], strip_sem.at[0, k], strip_sem.at[1, k], "dev", d).wait_recv()
    total = strip_in[0]
    for k in range(1, D):
        total = total + strip_in[k]
    ghost[...] = jnp.transpose(jnp.concatenate([total, jnp.zeros((112, 128), F32)], axis=0))

    spread_off = iota((128, 128), 1) - 3 * iota((128, 128), 0)
    fine_ghost = select_dot(split3(ghost[...]), one_hot((spread_off >= 0) & (spread_off < 3)))
    open_rows = ((lane >= 3) | (d != 0)) & ((lane < NR + 3) | (d != D - 1)) & (lane < NR + 6)
    n_c, n_x, n_w, n_y, n_s = (jnp.concatenate([coef[i]] * 2, axis=0) for i in range(5))

    def along(u, add):
        if u is not None:
            add += n_c * u + n_y * pltpu.roll(u, 127, 1) + n_s * pltpu.roll(u, 1, 1)
        return jnp.where(open_rows, add, 0.0)

    pack_off = iota((128, 128), 1) - 3 * (iota((128, 128), 0) - 3)
    packed = []
    for side, near, far in ((0, n_w, n_x), (1, n_x, n_w)):
        g_side = jnp.concatenate([fine_ghost[48 * a + C * side : 48 * a + C * side + C] for a in range(2)], axis=0)
        lines = response(g_side, near, far, along)
        packed.append(
            sum(
                select_dot(split2(v), one_hot(pack_off == (k if side == 0 else 2 - k)))
                for k, v in enumerate(lines)
            )
        )
    fix_w[...] = packed[0]
    fix_e[...] = packed[1]

    def fix_cols(t, _):
        plane = pl.ds(pl.multiple_of(8 * t, 8), 8)
        w_fix, e_fix = fix_w[plane, :], fix_e[plane, :]
        for f in range(NR):
            res[f, plane, pl.ds(0, 128)] += jnp.where(lane < 3, pltpu.roll(w_fix, (128 - 3 * f) % 128, 1), 0.0)
            res[f, plane, pl.ds(256, 128)] += jnp.where(lane >= 125, pltpu.roll(e_fix, (125 - 3 * f) % 128, 1), 0.0)
        return 0

    lax.fori_loop(0, 6, fix_cols, 0)

    def store_rows(some):
        for r in some:
            cp = pltpu.make_async_copy(res.at[r], nout.at[:, r, :], row_sem.at[r])
            cp.start()
            outs.append(cp)

    store_rows(range(3, NR - 3))
    to_pair(1)
    to_pair(2)
    place(0)

    for e, end in ((0, 0), (1, D - 1)):

        @pl.when(d == end)
        def _(e=e, end=end):
            whole = edge[e]
            for k in range(1, D):
                s = (end + k) % D
                remote(edge.at[e], edge_in.at[s], edge_sem.at[0, e], edge_sem.at[1, s], "dev", end).wait_recv()
            for k in range(1, D):
                whole = whole + edge_in[(end + k) % D]
            off = iota((TC, NC), 1) - 3 * iota((TC, NC), 0)
            spread = jnp.where((off >= 0) & (off < 3), 1.0, 0.0).astype(BF16)
            fine[...] = sum(
                jnp.dot(part, spread, preferred_element_type=F32) for part in split3(whole)
            )

        @pl.when(d != end)
        def _(e=e, end=end):
            remote(edge.at[e], edge_in.at[d], edge_sem.at[0, e], edge_sem.at[1, d], "dev", end).wait_send()


    for e, end in ((0, 0), (1, D - 1)):

        @pl.when(d == end)
        def _(e=e):
            n3 = [jnp.concatenate([v] * 3, axis=1) for v in (n_c, n_x, n_w, n_y, n_s)]
            at = iota((PLANES, NC), 1)

            def over(u, add):
                if u is None:
                    return add
                right = jnp.where(at == NC - 1, 0.0, pltpu.roll(u, NC - 1, 1))
                left = jnp.where(at == 0, 0.0, pltpu.roll(u, 1, 1))
                return n3[0] * u + n3[1] * right + n3[2] * left + add

            near, far = (n3[4], n3[3]) if e == 0 else (n3[3], n3[4])
            for k, v in enumerate(response(fine[...], near, far, over)):
                res[k if e == 0 else NR - 1 - k] += v

    store_rows([0, 1, 2, NR - 3, NR - 2, NR - 1])
    place(1)
    place(2)
    for cp in sends:
        cp.wait_send()
    for cp in outs:
        cp.wait()


def shards(parent, nest, anchor, diffusion, courant):
    any_space = pl.BlockSpec(memory_space=pl.ANY)
    scalars = pl.BlockSpec(memory_space=pltpu.SMEM)
    dma = pltpu.SemaphoreType.DMA
    vmem = pltpu.VMEM
    pout, nout = pl.pallas_call(
        kernel,
        out_shape=(
            pltpu.VMEM((C, TR, TC), F32),
            pltpu.VMEM((PLANES, NR, NC), F32),
        ),
        in_specs=[scalars] * 3 + [pl.BlockSpec(memory_space=pltpu.HBM)] * 2,
        out_specs=(any_space, any_space),
        scratch_shapes=[
            vmem((NR + 6, PLANES, NC), F32),
            vmem((NR, PLANES, NC), F32),
            vmem((C, TR, TC), F32),
            vmem((2, C, 8, TC), F32),
            vmem((2, TR, 128), F32),
            vmem((2, TR, 128), F32),
            vmem((G, TR + PLANES, 128), F32),
            vmem((G, TR + PLANES, 128), F32),
            vmem((LEAD + G * TR + 32, 128), F32),
            vmem((D, 16, 128), F32),
            vmem((D, 16, 128), F32),
            vmem((2, PLANES, 128), F32),
            vmem((D, PLANES, 128), F32),
            vmem((128, 128), F32),
            vmem((PLANES, NC), F32),
            vmem((5, C, 128), F32),
            vmem((128, NC), F32),
            vmem((TR, 128), F32),
            vmem((2, 8, 128), F32),
            vmem((C, 128), F32),
            vmem((2, C, 128), F32),
            vmem((3 * (TR + 16), 128), F32),
            vmem((TR, 128), F32),
            vmem((PLANES, 128), F32),
            vmem((PLANES, 128), F32),
            vmem((3, 2, 8, 8, TC), F32),
            *[vmem((NESTS, 4, 8, TC), F32)] * 3,
            vmem((3, D, 4, 8, TC), F32),
            *[vmem((32, 2, 4, 8, TC), F32)] * 3,
            vmem((8 * TR, TC), F32),
            vmem((C, TR, TC), F32),
            pltpu.SMEM((8,), I32),
            dma((NR,)),
            dma((4,)),
            dma((2, 10)),
            dma((2, G)),
            dma((2, D)),
            dma((2, D)),
            dma((2, 3, G)),
            dma((2, 3, D)),
            dma((2, 3)),
        ],
        compiler_params=pltpu.CompilerParams(
            collective_id=0, has_side_effects=True, vmem_limit_bytes=52 * 1024 * 1024
        ),
    )(anchor.T, diffusion, courant, pltpu.with_memory_space_constraint(parent, pltpu.HBM), pltpu.with_memory_space_constraint(nest.reshape(PLANES, NR, NC), pltpu.HBM))
    return pout, nout.reshape(2, C, NR, NC)


def solution(mesh):
    placed = (P(None, "grp", "dev"), P("grp", None, "dev", None), P(), P(), P())
    return jax.shard_map(
        shards,
        mesh=mesh,
        in_specs=placed,
        out_specs=(P(None, "grp", "dev"), P("grp", None, "dev", None)),
        check_vma=False,
    )
```
